256 devices in a mesh: gz: 64 (over x, y, z_hi, core), gy: 4 (over z_lo).
Axes of the slice: x: 4, y: 4, z: 8 (z_hi: 2, z_lo: 4; z = z_hi * 4 + z_lo), core: 2. Of those that a mesh axis runs over, the one named last changes fastest.
Arguments:
- velocity: float32 [2, 2, 1536, 7680], P(None, None, 'gz', 'gy'), may hold values from -0.15625 to 0.15625
- vorticity: float32 [2, 2, 1536, 7680], P(None, None, 'gz', 'gy'), may hold values from -0.15625 to 0.15625
Outputs:
- criterion: float32 [2, 4, 1920, 1536], P(None, None, 'gz', 'gy')
The draws below stay inside these ranges and needn't reach their ends.
All inputs are finite; a program needn't handle non-finite values.
Results may differ from the reference program's by a relative error of at most 0.0003.
Values sent between devices are 32-bit elements; how exact they have to be, the bound alone decides.
No kernel may reach another device: no remote copies, remote signals or barrier semaphores. Data moves between devices by JAX's collectives and lax.ppermute only.
A program may use at most 128 MiB of HBM per device.

```python
import math
import jax
import jax.numpy as jnp
from jax import lax

NY = 1536
NZ = 7680
KX = 2
N_GY = 4


def shard_levels(stream_key, shape, cuts, low, high):
    loudness = 1.0
    for axis_at, shards_of in cuts:
        draws = jax.random.uniform(jax.random.fold_in(jax.random.fold_in(stream_key, 6), axis_at), (shards_of,), jnp.float32, low / len(cuts), high / len(cuts))
        loudness = loudness * jnp.repeat(jnp.exp(draws), shape[axis_at] // shards_of).reshape((-1,) + (1,) * (len(shape) - 1 - axis_at))
    return loudness


def normal_values(own_key, extent, deviation, most, cuts=(), kind=jnp.bfloat16):
    array = jax.random.normal(own_key, extent, jnp.float32) * deviation
    if len(cuts) > 0:
        array = shard_levels(own_key, extent, cuts, -0.22, 0.18) * array
    return jnp.clip(array, min=-most, max=most).astype(kind)


def setup_inputs(seed: int = 0) -> dict:
    seeds = jax.random.split(jax.random.key(seed), 3)
    return {
        "velocity": normal_values(seeds[0], (2, KX, NY, NZ), NY ** -0.5, 0.15625, ((2, 64), (3, 4)), jnp.float32),
        "vorticity": normal_values(seeds[1], (2, KX, NY, NZ), NY ** -0.5, 0.15625, ((2, 64), (3, 4)), jnp.float32),
    }


def cheb_tables(order):
    points = jnp.arange(order, dtype=jnp.int32)
    turns = (points[None, :] * (2 * points[:, None] + 1)) % (4 * order)
    angle = turns.astype(jnp.float32) * (math.pi / (2 * order))
    degree = points[None, :].astype(jnp.float32)
    return jnp.cos(angle), -(math.pi / order) * degree * jnp.sin(angle)


def spanwise(index):
    signed = jnp.where(index < NZ // 2, index, index - NZ)
    return signed.astype(jnp.float32) * (2.0 / NZ)


def velocities(wave_x, wave_z, growth, vortex):
    inverse = 1.0 / (wave_x * wave_x + wave_z * wave_z)
    first_re = wave_x * growth[0] - wave_z * vortex[0]
    first_im = wave_x * growth[1] - wave_z * vortex[1]
    second_re = wave_z * growth[0] + wave_x * vortex[0]
    second_im = wave_z * growth[1] + wave_x * vortex[1]
    stream = (-first_im * inverse, first_re * inverse)
    across = (-second_im * inverse, second_re * inverse)
    return stream, across


def wall_slope(field):
    widths = [(0, 0)] * (field.ndim - 1) + [(1, 1)]
    padded = jnp.pad(field, widths)
    return 0.5 * (padded[..., 2:] - padded[..., :-2])


def q_value(wave_x, wave_z, normal, growth, stream, across, stream_grad, across_grad):
    total = wave_x * wave_x * (stream[0] * stream[0] + stream[1] * stream[1])
    total = total + growth[0] * growth[0] + growth[1] * growth[1]
    total = total + wave_z * wave_z * (across[0] * across[0] + across[1] * across[1])
    total = total + 2.0 * wave_x * (stream_grad[1] * normal[0] - stream_grad[0] * normal[1])
    total = total + 2.0 * wave_x * wave_z * (stream[0] * across[0] + stream[1] * across[1])
    total = total + 2.0 * wave_z * (normal[0] * across_grad[1] - normal[1] * across_grad[0])
    squares = stream[0] * stream[0] + stream[1] * stream[1] + normal[0] * normal[0] + normal[1] * normal[1]
    squares = squares + across[0] * across[0] + across[1] * across[1]
    gradient = (wave_x * wave_x + wave_z * wave_z) * squares
    gradient = gradient + stream_grad[0] * stream_grad[0] + stream_grad[1] * stream_grad[1]
    gradient = gradient + growth[0] * growth[0] + growth[1] * growth[1]
    gradient = gradient + across_grad[0] * across_grad[0] + across_grad[1] * across_grad[1]
    return 0.25 * (gradient - total)


def reference(velocity, vorticity):
    values, slopes = cheb_tables(NY)
    wave_z = spanwise(jnp.arange(NZ, dtype=jnp.int32))[:, None]

    def one_mode(inputs):
        index, field_v, field_o = inputs
        wave_x = (index + 1).astype(jnp.float32) / KX
        normal = jnp.einsum("cnz,jn->czj", field_v, values, precision=lax.Precision.HIGHEST)
        growth = jnp.einsum("cnz,jn->czj", field_v, slopes, precision=lax.Precision.HIGHEST)
        vortex = jnp.einsum("cnz,jn->czj", field_o, values, precision=lax.Precision.HIGHEST)
        stream, across = velocities(wave_x, wave_z, growth, vortex)
        stream_grad = (wall_slope(stream[0]), wall_slope(stream[1]))
        across_grad = (wall_slope(across[0]), wall_slope(across[1]))
        return q_value(wave_x, wave_z, normal, growth, stream, across, stream_grad, across_grad)

    result = lax.map(one_mode, (jnp.arange(KX, dtype=jnp.int32), jnp.moveaxis(velocity, 1, 0), jnp.moveaxis(vorticity, 1, 0)))
    return result.reshape(KX, N_GY, NZ // N_GY, NY)
```

```python
import math

import jax
import jax.numpy as jnp
from jax import lax
from jax.experimental import pallas as pl
from jax.experimental.pallas import tpu as pltpu
from jax.sharding import PartitionSpec as P

NY = 1536
NZ = 7680
KX = 2
HALF = NY // 2
SLOT = 32
LANES = 128
GROUPS = ((0,), (1,))
LIMIT = 48 * 1024 * 1024


def spanwise(index):
    signed = jnp.where(index < NZ // 2, index, index - NZ)
    return signed.astype(jnp.float32) * (2.0 / NZ)


def pack_kernel(cols, v_ref, o_ref, out_ref):
    peers, rows, width = out_ref.shape
    lane = lax.broadcasted_iota(jnp.int32, (8, LANES), 1)
    chunks = v_ref.shape[-1] // LANES
    for i in range(width // LANES):
        for t in range(rows // 8):
            at = pl.ds(8 * t, 8)
            for a in range(peers):
                k, off = divmod(cols * a, LANES)
                merged = None
                for g in range(4):
                    ref, c = (v_ref, o_ref)[g // 2], g % 2
                    piece = ref[c, i, at, pl.ds(LANES * k, LANES)]
                    if off + cols > LANES:
                        after = ref[c, i, at, pl.ds(LANES * ((k + 1) % chunks), LANES)]
                        piece = jnp.where(lane >= off, piece, after)
                    shift = (SLOT * g - off) % LANES
                    if shift:
                        piece = pltpu.roll(piece, shift, 1)
                    merged = piece if merged is None else jnp.where(lane >= SLOT * g, piece, merged)
                out_ref[a, at, pl.ds(LANES * i, LANES)] = merged


def pack(velocity, vorticity, modes, peers):
    _, _, rows, span = velocity.shape
    width = LANES * len(modes)
    block = pl.BlockSpec((2, len(modes), rows, span), lambda i: (0, modes[0] // len(modes), 0, 0))
    return pl.pallas_call(
        lambda *refs: pack_kernel(span // peers, *refs),
        grid=(1,),
        in_specs=[block, block],
        out_specs=pl.BlockSpec((peers, rows, width), lambda i: (0, 0, 0)),
        out_shape=jax.ShapeDtypeStruct((peers, rows, width), jnp.float32),
        compiler_params=pltpu.CompilerParams(vmem_limit_bytes=LIMIT),
        name="pack",
    )(velocity, vorticity)


def table_kernel(base_ref, hi_ref, lo_ref):
    c, s = base_ref[0, 0], base_ref[0, 1]
    turn_c, turn_s = base_ref[0, 2], base_ref[0, 3]
    for q in range(HALF // LANES):
        high = c.astype(jnp.bfloat16)
        hi_ref[0, :, pl.ds(LANES * q, LANES)] = high
        lo_ref[0, :, pl.ds(LANES * q, LANES)] = (c - high.astype(jnp.float32)).astype(jnp.bfloat16)
        c, s = c * turn_c - s * turn_s, s * turn_c + c * turn_s


def tables():
    point = jnp.arange(HALF, dtype=jnp.int32)[:, None]
    first = 2 * jnp.arange(LANES, dtype=jnp.int32)[None, :]
    turn = jnp.full((1, LANES), 2 * LANES, jnp.int32)

    def angle(degree):
        return (degree * (2 * point + 1) % (4 * NY)).astype(jnp.float32) * (math.pi / (2 * NY))

    degrees = jnp.stack([angle(first), angle(first + 1)])
    turns = jnp.broadcast_to(angle(turn), degrees.shape)
    base = jnp.stack([jnp.cos(degrees), jnp.sin(degrees), jnp.cos(turns), jnp.sin(turns)], axis=1)
    rows = 64
    shape = jax.ShapeDtypeStruct((2, HALF, HALF), jnp.bfloat16)
    return pl.pallas_call(
        table_kernel,
        grid=(2, HALF // rows),
        in_specs=[pl.BlockSpec((1, 4, rows, LANES), lambda p, i: (p, 0, i, 0))],
        out_specs=[pl.BlockSpec((1, rows, HALF), lambda p, i: (p, i, 0))] * 2,
        out_shape=[shape, shape],
        compiler_params=pltpu.CompilerParams(vmem_limit_bytes=LIMIT),
        name="tables",
    )(base)


def degree_weights():
    degree = jnp.arange(NY, dtype=jnp.int32).reshape(HALF, 2).T.astype(jnp.float32)
    scaled = degree * (math.pi / NY)
    stretch = scaled * jnp.sin(scaled)
    edge = -0.5 * scaled * jnp.sin(0.5 * scaled)
    both = jnp.stack([stretch, edge], axis=1)
    return jnp.broadcast_to(both[..., None], (2, 2, HALF, LANES))


def criterion_kernel(x_ref, hi_ref, lo_ref, weight_ref, wave_ref, flip_ref, out_ref, low_ref, top_ref):
    lane = lax.broadcasted_iota(jnp.int32, (1, LANES), 1)
    normal = lane < 2 * SLOT
    for i in range(x_ref.shape[1] // LANES):
        wave = wave_ref[i][:1]
        halves = []
        for parity in range(2):
            x = x_ref[pl.ds(parity, HALF, stride=2), pl.ds(LANES * i, LANES)]
            scaled = x * jnp.where(normal, wave + weight_ref[parity, 0], 1.0)
            edge = jnp.sum(x * weight_ref[parity, 1], axis=0, keepdims=True)
            high = scaled.astype(jnp.bfloat16)
            low = (scaled - high.astype(jnp.float32)).astype(jnp.bfloat16)
            wide = jnp.concatenate([high, low], axis=1)
            first = jnp.dot(hi_ref[parity], wide, preferred_element_type=jnp.float32)
            second = jnp.dot(lo_ref[parity], high, preferred_element_type=jnp.float32)
            total = first[:, :LANES] + first[:, LANES:] + second
            row = lax.broadcasted_iota(jnp.int32, (HALF, LANES), 0)
            halves.append(total + jnp.where((row == 0) & normal, edge, 0.0))
        low_ref[pl.ds(8, HALF), :] = halves[0] + halves[1]
        top_ref[pl.ds(8, HALF), :] = halves[0] - halves[1]
        outside = jnp.zeros((8, LANES), jnp.float32)
        low_ref[pl.ds(0, 8), :] = outside
        top_ref[pl.ds(0, 8), :] = outside
        low_ref[pl.ds(8 + HALF, 1), :] = top_ref[pl.ds(7 + HALF, 1), :]
        top_ref[pl.ds(8 + HALF, 1), :] = low_ref[pl.ds(7 + HALF, 1), :]
        inverse = 0.25 / wave
        for b in range(HALF // LANES):
            parts = []
            for ref in (low_ref, top_ref):
                here = ref[pl.ds(8 + LANES * b, LANES), :]
                slope = 0.5 * (ref[pl.ds(9 + LANES * b, LANES), :] - ref[pl.ds(7 + LANES * b, LANES), :])
                square = here * here
                parts.append(jnp.where(normal, square * inverse, 0.25 * square + slope * slope * inverse))
            folded = jnp.where(normal, parts[0], parts[1])
            folded = folded + pltpu.roll(jnp.where(normal, parts[1], parts[0]), 2 * SLOT, 1)
            folded = folded + pltpu.roll(folded, SLOT, 1)
            turned = folded.T
            below = turned[SLOT : 2 * SLOT]
            above = jnp.dot(
                turned[3 * SLOT : 4 * SLOT], flip_ref[...],
                precision=lax.Precision.HIGHEST, preferred_element_type=jnp.float32,
            )
            for first_point, value in ((LANES * b, below), (NY - LANES * (b + 1), above)):
                peer, at = divmod(first_point, out_ref.shape[-1])
                out_ref[peer, pl.ds(SLOT * i, SLOT), pl.ds(at, LANES)] = value


def criterion(field, high, low, weights, wave, peers):
    width = field.shape[-1]
    modes = width // LANES
    flip = jnp.fliplr(jnp.eye(LANES, dtype=jnp.float32))
    return pl.pallas_call(
        criterion_kernel,
        out_shape=jax.ShapeDtypeStruct((peers, SLOT * modes, NY // peers), jnp.float32),
        scratch_shapes=[pltpu.VMEM((HALF + 16, LANES), jnp.float32)] * 2,
        compiler_params=pltpu.CompilerParams(vmem_limit_bytes=LIMIT),
        name="criterion",
    )(field.reshape(NY, width), high, low, weights, wave, flip)


def local(velocity, vorticity):
    spans = lax.axis_size("gz")
    walls = lax.axis_size("gy")
    columns = NZ // (spans * walls)
    received = []
    for modes in GROUPS:
        sent = pack(velocity, vorticity, modes, spans)
        received.append(lax.all_to_all(sent, "gz", split_axis=0, concat_axis=0, tiled=True))
    high, low = tables()
    weights = degree_weights()
    index = (
        lax.axis_index("gy") * (NZ // walls)
        + lax.axis_index("gz") * columns
        + jnp.arange(LANES, dtype=jnp.int32) % SLOT
    )
    wave_z = spanwise(index)
    wave_x = (jnp.arange(KX, dtype=jnp.int32) + 1).astype(jnp.float32) / KX
    wave = wave_x[:, None] * wave_x[:, None] + wave_z[None, :] * wave_z[None, :]
    wave = jnp.broadcast_to(wave[:, None, :], (KX, 8, LANES))
    results = []
    for modes, field in zip(GROUPS, received):
        part = criterion(field, high, low, weights, wave[modes[0] : modes[-1] + 1], walls)
        part = lax.all_to_all(part, "gy", split_axis=0, concat_axis=0, tiled=True)
        part = part.reshape(walls, len(modes), SLOT, NY // walls)[:, :, :columns]
        results.append(jnp.moveaxis(part, 1, 0))
    return jnp.concatenate(results, axis=0)


def solution(mesh):
    placed = P(None, None, "gz", "gy")
    return jax.shard_map(
        local, mesh=mesh, in_specs=(placed, placed), out_specs=placed, check_vma=False
    )
```

```python
import math

import jax
import jax.numpy as jnp
from jax import lax
from jax.experimental import pallas as pl
from jax.experimental.pallas import tpu as pltpu
from jax.sharding import Mesh
from jax.sharding import PartitionSpec as P

NY = 1536
NZ = 7680
KX = 2
HALF = NY // 2
SLOT = 32
LANES = 128
LIMIT = 24 * 1024 * 1024
SPANS = ("x", "y", "half", "core")
ROUTE = ("half", "y", "x", "core")
SIZES = {"x": 4, "y": 4, "half": 2, "core": 2}


def routes():
    places = []
    for a in range(math.prod(SIZES.values())):
        rest, at = a, {}
        for name in reversed(SPANS):
            rest, at[name] = divmod(rest, SIZES[name])
        place = 0
        for name in ROUTE:
            place = place * SIZES[name] + at[name]
        places.append(place)
    return places


def spanwise(index):
    signed = jnp.where(index < NZ // 2, index, index - NZ)
    return signed.astype(jnp.float32) * (2.0 / NZ)


def pack_kernel(places, cols, v_hbm, o_hbm, out_ref, v_buf, o_buf, sems):
    _, modes, rows, span = v_buf.shape
    chunks = span // LANES
    copies = []
    for t in range(rows // 8):
        at = pl.ds(8 * t, 8)
        pair = [
            pltpu.make_async_copy(src.at[:, :, at, :], dst.at[:, :, at, :], sems.at[t, f])
            for f, (src, dst) in enumerate(((v_hbm, v_buf), (o_hbm, o_buf)))
        ]
        for copy in pair:
            copy.start()
        copies.append(pair)
    lane = lax.broadcasted_iota(jnp.int32, (8, LANES), 1)
    for t in range(rows // 8):
        at = pl.ds(8 * t, 8)
        for copy in copies[t]:
            copy.wait()
        turned = {}

        def tile(m, g, k):
            if (m, g, k) not in turned:
                ref = (v_buf, o_buf)[g // 2]
                value = ref[g % 2, m, at, pl.ds(LANES * (k % chunks), LANES)]
                turned[m, g, k] = pltpu.roll(value, SLOT * g, 1) if g else value
            return turned[m, g, k]

        for a, place in enumerate(places):
            k, off = divmod(cols * a, LANES)
            own = (lane - off) & (LANES - 1)
            for m in range(modes):
                merged = [tile(m, 0, k + s) for s in range(2 if off + cols > LANES else 1)]
                for g in range(1, 4):
                    merged = [jnp.where(own >= SLOT * g, tile(m, g, k + s), v) for s, v in enumerate(merged)]
                value = merged[0]
                if len(merged) > 1:
                    value = jnp.where((own & (SLOT - 1)) < LANES - off, value, merged[1])
                out_ref[place, pl.ds(8 * t * modes + m, 8, stride=modes), :] = value


def pack(velocity, vorticity, places):
    _, modes, rows, span = velocity.shape
    peers = len(places)
    return pl.pallas_call(
        lambda *refs: pack_kernel(places, span // peers, *refs),
        in_specs=[pl.BlockSpec(memory_space=pltpu.HBM)] * 2,
        out_shape=jax.ShapeDtypeStruct((peers, rows * modes, LANES), jnp.float32),
        scratch_shapes=[pltpu.VMEM(velocity.shape, jnp.float32)] * 2
        + [pltpu.SemaphoreType.DMA((rows // 8, 2))],
        compiler_params=pltpu.CompilerParams(vmem_limit_bytes=LIMIT),
        name="pack",
    )(*(pltpu.with_memory_space_constraint(x, pltpu.HBM) for x in (velocity, vorticity)))


def table_kernel(base_ref, hi_ref, lo_ref):
    rows = 32

    def block(i, carry):
        at = pl.ds(pl.multiple_of(i * rows, rows), rows)
        for parity in range(2):
            c, s, turn_c, turn_s = (base_ref[parity, k, at, :] for k in range(4))
            for q in range(HALF // LANES):
                lanes = pl.ds(LANES * q, LANES)
                hi_ref[parity, at, lanes], lo_ref[parity, at, lanes] = halves_of(c)
                c, s = c * turn_c - s * turn_s, s * turn_c + c * turn_s
        return carry

    lax.fori_loop(0, HALF // rows, block, 0)


def tables():
    point = jnp.arange(HALF, dtype=jnp.int32)[:, None]
    first = 2 * jnp.arange(LANES, dtype=jnp.int32)[None, :]
    turn = jnp.full((1, LANES), 2 * LANES, jnp.int32)

    def angle(degree):
        return (degree * (2 * point + 1) % (4 * NY)).astype(jnp.float32) * (math.pi / (2 * NY))

    degrees = jnp.stack([angle(first), angle(first + 1)])
    turns = jnp.broadcast_to(angle(turn), degrees.shape)
    base = jnp.stack([jnp.cos(degrees), jnp.sin(degrees), jnp.cos(turns), jnp.sin(turns)], axis=1)
    return pl.pallas_call(
        table_kernel,
        out_shape=[jax.ShapeDtypeStruct((2, HALF, HALF), jnp.bfloat16)] * 2,
        compiler_params=pltpu.CompilerParams(vmem_limit_bytes=LIMIT),
        name="tables",
    )(base)


def factors(own, first):
    normal = own < 2 * SLOT
    wave_z = spanwise(first + own % SLOT)
    wave_x = (jnp.arange(KX, dtype=jnp.int32) + 1).astype(jnp.float32) / KX
    wave = wave_x[:, None] * wave_x[:, None] + wave_z[None, :] * wave_z[None, :]
    degree = jnp.arange(NY, dtype=jnp.int32).reshape(HALF, 2).T.astype(jnp.float32)
    scaled = degree * (math.pi / NY)
    stretch = (scaled * jnp.sin(scaled))[:, :, None]
    edge = (-0.5 * scaled * jnp.sin(0.5 * scaled))[:, :, None]
    by_degree = jnp.where(normal, jnp.stack([stretch, edge]), 0.0)
    shift = jnp.where(normal, wave, 1.0)
    square = jnp.where(normal, 0.25 / wave, 0.25)
    slope = jnp.where(normal, 0.0, 0.0625 / wave)
    rows = jnp.broadcast_to(jnp.stack([shift, square, slope], axis=1)[:, :, None, :], (KX, 3, 8, LANES))
    lane = jnp.arange(LANES, dtype=jnp.int32)
    part = jnp.arange(4, dtype=jnp.int32)
    pick = (own[None, :, None] % SLOT == lane % SLOT) & (lane // SLOT == part[:, None, None])
    flip = lane[:, None] + lane[None, :] == LANES - 1
    return by_degree, rows, pick.astype(jnp.bfloat16), flip.astype(jnp.bfloat16)


def halves_of(value):
    high = value.astype(jnp.bfloat16)
    return high, (value - high.astype(jnp.float32)).astype(jnp.bfloat16)


def product(a, b):
    return jnp.dot(a, b, preferred_element_type=jnp.float32)


def criterion_kernel(
    places, x_ref, hi_hbm, lo_hbm, degree_ref, rows_ref, pick_ref, flip_ref, out_ref,
    hi_ref, lo_ref, xh_ref, xl_ref, low_ref, top_ref, sems,
):
    copies = [
        pltpu.make_async_copy(src.at[parity], dst.at[parity], sems.at[parity, k])
        for parity in range(2)
        for k, (src, dst) in enumerate(((hi_hbm, hi_ref), (lo_hbm, lo_ref)))
    ]
    for copy in copies:
        copy.start()
    modes = x_ref.shape[0] // NY
    pair = 2 * NY // len(places)
    sums = []
    for parity in range(2):
        for m in range(modes):
            lanes = pl.ds(LANES * m, LANES)
            total = jnp.zeros((pair // 2, LANES), jnp.float32)
            shift = rows_ref[m, 0, :1]
            for c in range(NY // pair):
                at = pl.ds(c * pair // 2, pair // 2)
                first = places[2 * c] * (pair // 2) * modes + parity * modes + m
                x = x_ref[pl.ds(first, pair // 2, stride=2 * modes), :]
                total = total + x * degree_ref[1, parity, at, :]
                high, low = halves_of(x * (shift + degree_ref[0, parity, at, :]))
                xh_ref[parity, at, lanes] = high
                xl_ref[parity, at, lanes] = low
            sums.append(jnp.sum(total, axis=0, keepdims=True))
    for copy in copies:
        copy.wait()
    halves = []
    for parity in range(2):
        xh = xh_ref[parity]
        halves.append(
            product(hi_ref[parity], xh) + product(hi_ref[parity], xl_ref[parity]) + product(lo_ref[parity], xh)
        )
    low_ref[pl.ds(8, HALF), :] = halves[0] + halves[1]
    top_ref[pl.ds(8, HALF), :] = halves[0] - halves[1]
    for m in range(modes):
        lanes = pl.ds(LANES * m, LANES)
        even, odd = sums[m], sums[modes + m]
        low_ref[pl.ds(8, 1), lanes] = low_ref[pl.ds(8, 1), lanes] + (even + odd)
        top_ref[pl.ds(8, 1), lanes] = top_ref[pl.ds(8, 1), lanes] + (even - odd)
    outside = jnp.zeros((8, LANES * modes), jnp.float32)
    low_ref[pl.ds(0, 8), :] = outside
    top_ref[pl.ds(0, 8), :] = outside
    low_ref[pl.ds(8 + HALF, 1), :] = top_ref[pl.ds(7 + HALF, 1), :]
    top_ref[pl.ds(8 + HALF, 1), :] = low_ref[pl.ds(7 + HALF, 1), :]
    above = []
    for b in range(HALF // LANES):
        result = None
        for part in range(2 * modes):
            ref, m = (low_ref, top_ref)[part // modes], part % modes
            lanes = pl.ds(LANES * m, LANES)
            here = ref[pl.ds(8 + LANES * b, LANES), lanes]
            slope = ref[pl.ds(9 + LANES * b, LANES), lanes] - ref[pl.ds(7 + LANES * b, LANES), lanes]
            value = here * here * rows_ref[m, 1, :1] + slope * slope * rows_ref[m, 2, :1]
            high, low = halves_of(value)
            added = product(high, pick_ref[part]) + product(low, pick_ref[part])
            result = added if result is None else result + added
        turned = result.T
        peer, at = divmod(LANES * b, out_ref.shape[-1])
        out_ref[peer, :, pl.ds(at, LANES)] = turned[: SLOT * modes]
        high, low = halves_of(turned[SLOT * modes :])
        peer, at = divmod(NY - LANES * (b + 1), out_ref.shape[-1])
        out_ref[peer, :, pl.ds(at, LANES)] = product(high, flip_ref[...]) + product(low, flip_ref[...])


def criterion(field, high, low, numbers, places, peers):
    modes = field.shape[1] * len(places) // NY
    width = LANES * modes
    fast, slow = pl.BlockSpec(memory_space=pltpu.VMEM), pl.BlockSpec(memory_space=pltpu.HBM)
    call = pl.pallas_call(
        lambda *refs: criterion_kernel(places, *refs),
        in_specs=[fast, slow, slow, fast, fast, fast, fast],
        out_shape=jax.ShapeDtypeStruct((peers, SLOT * modes, NY // peers), jnp.float32),
        scratch_shapes=[pltpu.VMEM(high.shape, jnp.bfloat16)] * 2
        + [pltpu.VMEM((2, HALF, width), jnp.bfloat16)] * 2
        + [pltpu.VMEM((HALF + 16, width), jnp.float32)] * 2
        + [pltpu.SemaphoreType.DMA((2, 2))],
        compiler_params=pltpu.CompilerParams(vmem_limit_bytes=LIMIT),
        name="criterion",
    )
    high, low = (pltpu.with_memory_space_constraint(x, pltpu.HBM) for x in (high, low))
    return call(field.reshape(NY * modes, LANES), high, low, *numbers)


def local(velocity, vorticity):
    walls = lax.axis_size("gy")
    places = routes()
    columns = NZ // (len(places) * walls)
    sent = pack(velocity, vorticity, places)
    field = lax.all_to_all(sent, ROUTE, split_axis=0, concat_axis=0, tiled=True)
    high, low = tables()
    start = lax.axis_index(SPANS) * columns
    own = (jnp.arange(LANES, dtype=jnp.int32) - start) % LANES
    numbers = factors(own, lax.axis_index("gy") * (NZ // walls) + start)
    part = criterion(field, high, low, numbers, places, walls)
    part = lax.all_to_all(part, "gy", split_axis=0, concat_axis=0, tiled=True)
    part = part.reshape(walls, KX, SLOT, NY // walls)[:, :, :columns]
    return jnp.moveaxis(part, 1, 0)


def solution(mesh):
    fine = Mesh(mesh.devices.reshape(*SIZES.values(), -1), (*SIZES, "gy"))
    placed = P(None, None, SPANS, "gy")
    return jax.shard_map(
        local, mesh=fine, in_specs=(placed, placed), out_specs=placed, check_vma=False
    )
```

```python
import math

import jax
import jax.numpy as jnp
from jax import lax
from jax.experimental import pallas as pl
from jax.experimental.pallas import tpu as pltpu
from jax.sharding import Mesh
from jax.sharding import PartitionSpec as P

NY = 1536
NZ = 7680
KX = 2
HALF = NY // 2
SLOT = 32
LANES = 128
BLOCK = 384
LIMIT = 24 * 1024 * 1024
SPANS = ("x", "y", "half", "core")
ROUTE = ("half", "y", "x", "core")
SIZES = {"x": 4, "y": 4, "half": 2, "core": 2}


def routes():
    places = []
    for a in range(math.prod(SIZES.values())):
        rest, at = a, {}
        for name in reversed(SPANS):
            rest, at[name] = divmod(rest, SIZES[name])
        place = 0
        for name in ROUTE:
            place = place * SIZES[name] + at[name]
        places.append(place)
    return places


def spanwise(index):
    signed = jnp.where(index < NZ // 2, index, index - NZ)
    return signed.astype(jnp.float32) * (2.0 / NZ)


def pack_kernel(places, cols, v_hbm, o_hbm, out_hbm, v_buf, o_buf, out_ref, sems):
    _, modes, rows, span = v_buf.shape
    chunks = span // LANES
    copies = []
    for t in range(rows // 8):
        at = pl.ds(8 * t, 8)
        pair = [
            pltpu.make_async_copy(src.at[:, :, at, :], dst.at[:, :, at, :], sems.at[t, f])
            for f, (src, dst) in enumerate(((v_hbm, v_buf), (o_hbm, o_buf)))
        ]
        for copy in pair:
            copy.start()
        copies.append(pair)
    lane = lax.broadcasted_iota(jnp.int32, (8, LANES), 1)
    leaving = []
    for t in range(rows // 8):
        at = pl.ds(8 * t, 8)
        for copy in copies[t]:
            copy.wait()
        turned = {}

        def tile(m, g, k):
            if (m, g, k) not in turned:
                ref = (v_buf, o_buf)[g // 2]
                value = ref[g % 2, m, at, pl.ds(LANES * (k % chunks), LANES)]
                turned[m, g, k] = pltpu.roll(value, SLOT * g, 1) if g else value
            return turned[m, g, k]

        for a, place in enumerate(places):
            k, off = divmod(cols * a, LANES)
            own = (lane - off) & (LANES - 1)
            for m in range(modes):
                merged = [tile(m, 0, k + s) for s in range(2 if off + cols > LANES else 1)]
                for g in range(1, 4):
                    merged = [jnp.where(own >= SLOT * g, tile(m, g, k + s), v) for s, v in enumerate(merged)]
                value = merged[0]
                if len(merged) > 1:
                    value = jnp.where((own & (SLOT - 1)) < LANES - off, value, merged[1])
                out_ref[place, pl.ds(8 * t * modes + m, 8, stride=modes), :] = value
        done = pl.ds(8 * t * modes, 8 * modes)
        leaving.append(pltpu.make_async_copy(out_ref.at[:, done, :], out_hbm.at[:, done, :], sems.at[t, 2]))
        leaving[-1].start()
    for copy in leaving:
        copy.wait()


def pack(velocity, vorticity, places):
    _, modes, rows, span = velocity.shape
    peers = len(places)
    return pl.pallas_call(
        lambda *refs: pack_kernel(places, span // peers, *refs),
        in_specs=[pl.BlockSpec(memory_space=pltpu.HBM)] * 2,
        out_specs=pl.BlockSpec(memory_space=pltpu.HBM),
        out_shape=jax.ShapeDtypeStruct((peers, rows * modes, LANES), jnp.float32),
        scratch_shapes=[pltpu.VMEM(velocity.shape, jnp.float32)] * 2
        + [pltpu.VMEM((peers, rows * modes, LANES), jnp.float32), pltpu.SemaphoreType.DMA((rows // 8, 3))],
        compiler_params=pltpu.CompilerParams(vmem_limit_bytes=LIMIT),
        name="pack",
    )(*(pltpu.with_memory_space_constraint(x, pltpu.HBM) for x in (velocity, vorticity)))


def table_kernel(base_ref, hi_ref, lo_ref):
    rows = 32

    def block(i, carry):
        at = pl.ds(pl.multiple_of(i * rows, rows), rows)
        for parity in range(2):
            c, s, turn_c, turn_s = (base_ref[parity, k, at, :] for k in range(4))
            for q in range(HALF // LANES):
                lanes = pl.ds(LANES * q, LANES)
                hi_ref[parity, at, lanes], lo_ref[parity, at, lanes] = halves_of(c)
                c, s = c * turn_c - s * turn_s, s * turn_c + c * turn_s
        return carry

    lax.fori_loop(0, HALF // rows, block, 0)


def tables():
    point = jnp.arange(HALF, dtype=jnp.int32)[:, None]
    first = 2 * jnp.arange(LANES, dtype=jnp.int32)[None, :]
    turn = jnp.full((1, LANES), 2 * LANES, jnp.int32)

    def angle(degree):
        return (degree * (2 * point + 1) % (4 * NY)).astype(jnp.float32) * (math.pi / (2 * NY))

    degrees = jnp.stack([angle(first), angle(first + 1)])
    turns = jnp.broadcast_to(angle(turn), degrees.shape)
    base = jnp.stack([jnp.cos(degrees), jnp.sin(degrees), jnp.cos(turns), jnp.sin(turns)], axis=1)
    return pl.pallas_call(
        table_kernel,
        out_shape=[jax.ShapeDtypeStruct((2, HALF, HALF), jnp.bfloat16)] * 2,
        compiler_params=pltpu.CompilerParams(vmem_limit_bytes=LIMIT),
        name="tables",
    )(base)


def factors(own, first):
    normal = own < 2 * SLOT
    wave_z = spanwise(first + own % SLOT)
    wave_x = (jnp.arange(KX, dtype=jnp.int32) + 1).astype(jnp.float32) / KX
    wave = wave_x[:, None] * wave_x[:, None] + wave_z[None, :] * wave_z[None, :]
    degree = jnp.arange(NY, dtype=jnp.int32).reshape(HALF, 2).T.astype(jnp.float32)
    scaled = degree * (math.pi / NY)
    stretch = (scaled * jnp.sin(scaled))[:, :, None]
    edge = (-0.5 * scaled * jnp.sin(0.5 * scaled))[:, :, None]
    by_degree = jnp.where(normal, jnp.stack([stretch, edge]), 0.0)
    shift = jnp.where(normal, wave, 1.0)
    size = jnp.where(normal, 0.5 * lax.rsqrt(wave), 0.5)
    slope = jnp.where(normal, 0.0, 0.25 / wave)
    rows = jnp.broadcast_to(jnp.stack([shift * size, size, slope], axis=1)[:, :, None, :], (KX, 3, 8, LANES))
    lane = jnp.arange(LANES, dtype=jnp.int32)
    part = jnp.arange(2 * KX, dtype=jnp.int32)
    pick = (own[None, :, None] % SLOT == lane % SLOT) & (lane // SLOT == part[:, None, None])
    pick = pick.reshape(2 * KX * LANES, LANES)
    flip = lane[:, None] + lane[None, :] == LANES - 1
    return by_degree, rows, pick.astype(jnp.bfloat16), flip.astype(jnp.bfloat16)


def halves_of(value):
    high = value.astype(jnp.bfloat16)
    return high, (value - high.astype(jnp.float32)).astype(jnp.bfloat16)


def product(a, b):
    return jnp.dot(a, b, preferred_element_type=jnp.float32)


def criterion_kernel(
    places, x_ref, hi_hbm, lo_hbm, degree_ref, rows_ref, pick_ref, flip_ref, out_ref,
    hi_ref, lo_ref, xh_ref, xl_ref, low_ref, top_ref, vh_ref, vl_ref, res_ref, sems,
):
    copies = [
        [
            pltpu.make_async_copy(src.at[:, at, :], dst.at[:, at, :], sems.at[b, k])
            for k, (src, dst) in enumerate(((hi_hbm, hi_ref), (lo_hbm, lo_ref)))
        ]
        for b, at in enumerate(pl.ds(start, BLOCK) for start in range(0, HALF, BLOCK))
    ]
    for copy in sum(copies, []):
        copy.start()
    modes = x_ref.shape[0] // NY
    pair = 2 * NY // len(places)
    half = pair // 2
    totals = [jnp.zeros((half, LANES), jnp.float32) for _ in range(2 * modes)]
    for parity in range(2):
        for m in range(modes):
            lanes = pl.ds(LANES * m, LANES)
            shift, size = rows_ref[m, 0, :1], rows_ref[m, 1, :1]
            for row in range(0, HALF, half):
                at = pl.ds(row, half)
                first = places[2 * row // half] * half * modes + parity * modes + m
                x = x_ref[pl.ds(first, half, stride=2 * modes), :]
                totals[parity * modes + m] = totals[parity * modes + m] + x * degree_ref[1, parity, at, :]
                high, low = halves_of(x * (shift + size * degree_ref[0, parity, at, :]))
                xh_ref[parity, at, lanes] = high
                xl_ref[parity, at, lanes] = low
    outside = jnp.zeros((8, LANES * modes), jnp.float32)
    low_ref[pl.ds(0, 8), :] = outside
    top_ref[pl.ds(0, 8), :] = outside

    def values(start, size):
        at = pl.ds(start, size)
        for part in range(2 * modes):
            ref, m = (low_ref, top_ref)[part // modes], part % modes
            lanes = pl.ds(LANES * m, LANES)
            here = ref[pl.ds(8 + start, size), lanes]
            slope = ref[pl.ds(9 + start, size), lanes] - ref[pl.ds(7 + start, size), lanes]
            high, low = halves_of(here * here + slope * slope * rows_ref[m, 2, :1])
            vh_ref[at, pl.ds(LANES * part, LANES)] = high
            vl_ref[at, pl.ds(LANES * part, LANES)] = low
        res_ref[at, :] = product(vh_ref[at, :], pick_ref[...]) + product(vl_ref[at, :], pick_ref[...])

    done = 0
    for start in range(0, HALF, BLOCK):
        at = pl.ds(start, BLOCK)
        for copy in copies[start // BLOCK]:
            copy.wait()
        halves = []
        for parity in range(2):
            xh = xh_ref[parity]
            halves.append(
                product(hi_ref[parity, at, :], xh) + product(hi_ref[parity, at, :], xl_ref[parity]) + product(lo_ref[parity, at, :], xh)
            )
        low_ref[pl.ds(8 + start, BLOCK), :] = halves[0] + halves[1]
        top_ref[pl.ds(8 + start, BLOCK), :] = halves[0] - halves[1]
        if start == 0:
            for m in range(modes):
                lanes = pl.ds(LANES * m, LANES)
                even, odd = (
                    rows_ref[m, 1, :1] * jnp.sum(totals[parity * modes + m], axis=0, keepdims=True) for parity in range(2)
                )
                low_ref[pl.ds(8, 1), lanes] = low_ref[pl.ds(8, 1), lanes] + (even + odd)
                top_ref[pl.ds(8, 1), lanes] = top_ref[pl.ds(8, 1), lanes] + (even - odd)
        if start + BLOCK == HALF:
            low_ref[pl.ds(8 + HALF, 1), :] = top_ref[pl.ds(7 + HALF, 1), :]
            top_ref[pl.ds(8 + HALF, 1), :] = low_ref[pl.ds(7 + HALF, 1), :]
        ready = start + BLOCK if start + BLOCK == HALF else start + BLOCK - 8
        while done < ready:
            size = min(LANES, ready - done)
            values(done, size)
            done += size
    above = []
    for b in range(HALF // LANES):
        turned = res_ref[pl.ds(LANES * b, LANES), :].T
        peer, at = divmod(LANES * b, out_ref.shape[-1])
        out_ref[peer, :, pl.ds(at, LANES)] = turned[: SLOT * modes]
        above.append(turned[SLOT * modes :])
    high, low = halves_of(jnp.concatenate(above, axis=0))
    above = product(high, flip_ref[...]) + product(low, flip_ref[...])
    for b in range(HALF // LANES):
        peer, at = divmod(NY - LANES * (b + 1), out_ref.shape[-1])
        out_ref[peer, :, pl.ds(at, LANES)] = above[SLOT * modes * b : SLOT * modes * (b + 1)]


def criterion(field, high, low, numbers, places, peers):
    modes = field.shape[1] * len(places) // NY
    width = LANES * modes
    fast, slow = pl.BlockSpec(memory_space=pltpu.VMEM), pl.BlockSpec(memory_space=pltpu.HBM)
    call = pl.pallas_call(
        lambda *refs: criterion_kernel(places, *refs),
        in_specs=[fast, slow, slow, fast, fast, fast, fast],
        out_shape=jax.ShapeDtypeStruct((peers, SLOT * modes, NY // peers), jnp.float32),
        scratch_shapes=[pltpu.VMEM(high.shape, jnp.bfloat16)] * 2
        + [pltpu.VMEM((2, HALF, width), jnp.bfloat16)] * 2
        + [pltpu.VMEM((HALF + 16, width), jnp.float32)] * 2
        + [pltpu.VMEM((HALF, 2 * width), jnp.bfloat16)] * 2
        + [pltpu.VMEM((HALF, LANES), jnp.float32), pltpu.SemaphoreType.DMA((HALF // BLOCK, 2))],
        compiler_params=pltpu.CompilerParams(vmem_limit_bytes=LIMIT),
        name="criterion",
    )
    high, low = (pltpu.with_memory_space_constraint(x, pltpu.HBM) for x in (high, low))
    return call(field.reshape(NY * modes, LANES), high, low, *numbers)


def local(velocity, vorticity):
    walls = lax.axis_size("gy")
    places = routes()
    columns = NZ // (len(places) * walls)
    sent = pack(velocity, vorticity, places)
    field = lax.all_to_all(sent, ROUTE, split_axis=0, concat_axis=0, tiled=True)
    high, low = tables()
    start = lax.axis_index(SPANS) * columns
    own = (jnp.arange(LANES, dtype=jnp.int32) - start) % LANES
    numbers = factors(own, lax.axis_index("gy") * (NZ // walls) + start)
    part = criterion(field, high, low, numbers, places, walls)
    part = lax.all_to_all(part, "gy", split_axis=0, concat_axis=0, tiled=True)
    part = part.reshape(walls, KX, SLOT, NY // walls)[:, :, :columns]
    return jnp.moveaxis(part, 1, 0)


def solution(mesh):
    fine = Mesh(mesh.devices.reshape(*SIZES.values(), -1), (*SIZES, "gy"))
    placed = P(None, None, SPANS, "gy")
    return jax.shard_map(
        local, mesh=fine, in_specs=(placed, placed), out_specs=placed, check_vma=False
    )
```

```python
import math

import jax
import jax.numpy as jnp
from jax import lax
from jax.experimental import pallas as pl
from jax.experimental.pallas import tpu as pltpu
from jax.sharding import Mesh
from jax.sharding import PartitionSpec as P

NY = 1536
NZ = 7680
KX = 2
HALF = NY // 2
SLOT = 32
LANES = 128
BLOCK = 384
LIMIT = 24 * 1024 * 1024
SPANS = ("x", "y", "half", "core")
ROUTE = ("half", "y", "x", "core")
SIZES = {"x": 4, "y": 4, "half": 2, "core": 2}


def routes():
    places = []
    for a in range(math.prod(SIZES.values())):
        rest, at = a, {}
        for name in reversed(SPANS):
            rest, at[name] = divmod(rest, SIZES[name])
        place = 0
        for name in ROUTE:
            place = place * SIZES[name] + at[name]
        places.append(place)
    return places


def spanwise(index):
    signed = jnp.where(index < NZ // 2, index, index - NZ)
    return signed.astype(jnp.float32) * (2.0 / NZ)


def pack_kernel(places, cols, v_hbm, o_hbm, out_hbm, v_buf, o_buf, out_ref, sems):
    _, modes, rows, span = v_buf.shape
    chunks = span // LANES
    copies = []
    for t in range(rows // 8):
        at = pl.ds(8 * t, 8)
        pair = [
            pltpu.make_async_copy(src.at[:, :, at, :], dst.at[:, :, at, :], sems.at[t, f])
            for f, (src, dst) in enumerate(((v_hbm, v_buf), (o_hbm, o_buf)))
        ]
        for copy in pair:
            copy.start()
        copies.append(pair)
    lane = lax.broadcasted_iota(jnp.int32, (8, LANES), 1)
    leaving = []
    for t in range(rows // 8):
        at = pl.ds(8 * t, 8)
        for copy in copies[t]:
            copy.wait()
        turned = {}

        def tile(m, g, k):
            if (m, g, k) not in turned:
                ref = (v_buf, o_buf)[g // 2]
                value = ref[g % 2, m, at, pl.ds(LANES * (k % chunks), LANES)]
                turned[m, g, k] = pltpu.roll(value, SLOT * g, 1) if g else value
            return turned[m, g, k]

        for a, place in enumerate(places):
            k, off = divmod(cols * a, LANES)
            own = (lane - off) & (LANES - 1)
            for m in range(modes):
                merged = [tile(m, 0, k + s) for s in range(2 if off + cols > LANES else 1)]
                for g in range(1, 4):
                    merged = [jnp.where(own >= SLOT * g, tile(m, g, k + s), v) for s, v in enumerate(merged)]
                value = merged[0]
                if len(merged) > 1:
                    value = jnp.where((own & (SLOT - 1)) < LANES - off, value, merged[1])
                out_ref[place, pl.ds(8 * t * modes + m, 8, stride=modes), :] = value
        done = pl.ds(8 * t * modes, 8 * modes)
        leaving.append(pltpu.make_async_copy(out_ref.at[:, done, :], out_hbm.at[:, done, :], sems.at[t, 2]))
        leaving[-1].start()
    for copy in leaving:
        copy.wait()


def pack(velocity, vorticity, places):
    _, modes, rows, span = velocity.shape
    peers = len(places)
    return pl.pallas_call(
        lambda *refs: pack_kernel(places, span // peers, *refs),
        in_specs=[pl.BlockSpec(memory_space=pltpu.HBM)] * 2,
        out_specs=pl.BlockSpec(memory_space=pltpu.HBM),
        out_shape=jax.ShapeDtypeStruct((peers, rows * modes, LANES), jnp.float32),
        scratch_shapes=[pltpu.VMEM(velocity.shape, jnp.float32)] * 2
        + [pltpu.VMEM((peers, rows * modes, LANES), jnp.float32), pltpu.SemaphoreType.DMA((rows // 8, 3))],
        compiler_params=pltpu.CompilerParams(vmem_limit_bytes=LIMIT),
        name="pack",
    )(*(pltpu.with_memory_space_constraint(x, pltpu.HBM) for x in (velocity, vorticity)))


def table_kernel(base_ref, hi_ref, lo_ref):
    rows = 32

    def block(i, carry):
        at = pl.ds(pl.multiple_of(i * rows, rows), rows)
        for parity in range(2):
            c, s, turn_c, turn_s = (base_ref[parity, k, at, :] for k in range(4))
            for q in range(HALF // LANES):
                lanes = pl.ds(LANES * q, LANES)
                hi_ref[parity, at, lanes], lo_ref[parity, at, lanes] = halves_of(c)
                c, s = c * turn_c - s * turn_s, s * turn_c + c * turn_s
        return carry

    lax.fori_loop(0, HALF // rows, block, 0)


def tables():
    point = jnp.arange(HALF, dtype=jnp.int32)[:, None]
    first = 2 * jnp.arange(LANES, dtype=jnp.int32)[None, :]
    turn = jnp.full((1, LANES), 2 * LANES, jnp.int32)

    def angle(degree):
        return (degree * (2 * point + 1) % (4 * NY)).astype(jnp.float32) * (math.pi / (2 * NY))

    degrees = jnp.stack([angle(first), angle(first + 1)])
    turns = jnp.broadcast_to(angle(turn), degrees.shape)
    base = jnp.stack([jnp.cos(degrees), jnp.sin(degrees), jnp.cos(turns), jnp.sin(turns)], axis=1)
    return pl.pallas_call(
        table_kernel,
        out_shape=[jax.ShapeDtypeStruct((2, HALF, HALF), jnp.bfloat16)] * 2,
        compiler_params=pltpu.CompilerParams(vmem_limit_bytes=LIMIT),
        name="tables",
    )(base)


def factors(own, first):
    normal = own < 2 * SLOT
    wave_z = spanwise(first + own % SLOT)
    wave_x = (jnp.arange(KX, dtype=jnp.int32) + 1).astype(jnp.float32) / KX
    wave = wave_x[:, None] * wave_x[:, None] + wave_z[None, :] * wave_z[None, :]
    degree = jnp.arange(NY, dtype=jnp.int32).reshape(HALF, 2).T.astype(jnp.float32)
    scaled = degree * (math.pi / NY)
    stretch = (scaled * jnp.sin(scaled))[:, :, None]
    edge = (-0.5 * scaled * jnp.sin(0.5 * scaled))[:, :, None]
    by_degree = jnp.where(normal, jnp.stack([stretch, edge]), 0.0)
    shift = jnp.where(normal, wave, 1.0)
    size = jnp.where(normal, 0.5 * lax.rsqrt(wave), 0.5)
    slope = jnp.where(normal, 0.0, 0.25 / wave)
    rows = jnp.broadcast_to(jnp.stack([shift * size, size, slope], axis=1)[:, :, None, :], (KX, 3, 8, LANES))
    lane = jnp.arange(LANES, dtype=jnp.int32)
    part = jnp.arange(2 * KX, dtype=jnp.int32)
    pick = (own[None, :, None] % SLOT == lane % SLOT) & (lane // SLOT == part[:, None, None])
    pick = pick.reshape(2 * KX * LANES, LANES)
    flip = lane[:, None] + lane[None, :] == LANES - 1
    return by_degree, rows, pick.astype(jnp.bfloat16), flip.astype(jnp.bfloat16)


def halves_of(value):
    high = value.astype(jnp.bfloat16)
    return high, (value - high.astype(jnp.float32)).astype(jnp.bfloat16)


def product(a, b):
    return jnp.dot(a, b, preferred_element_type=jnp.float32)


def criterion_kernel(
    places, peers, me_ref, x_ref, hi_hbm, lo_hbm, degree_ref, rows_ref, pick_ref, flip_ref, *refs
):
    outs, (hi_ref, lo_ref, xh_ref, xl_ref, low_ref, top_ref, vh_ref, vl_ref, res_ref, out_ref, sems) = (
        refs[:peers],
        refs[peers:],
    )
    copies = [
        [
            pltpu.make_async_copy(src.at[:, at, :], dst.at[:, at, :], sems.at[b, k])
            for k, (src, dst) in enumerate(((hi_hbm, hi_ref), (lo_hbm, lo_ref)))
        ]
        for b, at in enumerate(pl.ds(start, BLOCK) for start in range(0, HALF, BLOCK))
    ]
    for copy in sum(copies, []):
        copy.start()
    modes = x_ref.shape[0] // NY
    pair = 2 * NY // len(places)
    half = pair // 2
    totals = [jnp.zeros((half, LANES), jnp.float32) for _ in range(2 * modes)]
    for parity in range(2):
        for m in range(modes):
            lanes = pl.ds(LANES * m, LANES)
            shift, size = rows_ref[m, 0, :1], rows_ref[m, 1, :1]
            for row in range(0, HALF, half):
                at = pl.ds(row, half)
                first = places[2 * row // half] * half * modes + parity * modes + m
                x = x_ref[pl.ds(first, half, stride=2 * modes), :]
                totals[parity * modes + m] = totals[parity * modes + m] + x * degree_ref[1, parity, at, :]
                high, low = halves_of(x * (shift + size * degree_ref[0, parity, at, :]))
                xh_ref[parity, at, lanes] = high
                xl_ref[parity, at, lanes] = low
    outside = jnp.zeros((8, LANES * modes), jnp.float32)
    low_ref[pl.ds(0, 8), :] = outside
    top_ref[pl.ds(0, 8), :] = outside

    def values(start, size):
        at = pl.ds(start, size)
        for part in range(2 * modes):
            ref, m = (low_ref, top_ref)[part // modes], part % modes
            lanes = pl.ds(LANES * m, LANES)
            here = ref[pl.ds(8 + start, size), lanes]
            slope = ref[pl.ds(9 + start, size), lanes] - ref[pl.ds(7 + start, size), lanes]
            high, low = halves_of(here * here + slope * slope * rows_ref[m, 2, :1])
            vh_ref[at, pl.ds(LANES * part, LANES)] = high
            vl_ref[at, pl.ds(LANES * part, LANES)] = low
        res_ref[at, :] = product(vh_ref[at, :], pick_ref[...]) + product(vl_ref[at, :], pick_ref[...])

    done = 0
    for start in range(0, HALF, BLOCK):
        at = pl.ds(start, BLOCK)
        for copy in copies[start // BLOCK]:
            copy.wait()
        halves = []
        for parity in range(2):
            xh = xh_ref[parity]
            halves.append(
                product(hi_ref[parity, at, :], xh) + product(hi_ref[parity, at, :], xl_ref[parity]) + product(lo_ref[parity, at, :], xh)
            )
        low_ref[pl.ds(8 + start, BLOCK), :] = halves[0] + halves[1]
        top_ref[pl.ds(8 + start, BLOCK), :] = halves[0] - halves[1]
        if start == 0:
            for m in range(modes):
                lanes = pl.ds(LANES * m, LANES)
                even, odd = (
                    rows_ref[m, 1, :1] * jnp.sum(totals[parity * modes + m], axis=0, keepdims=True) for parity in range(2)
                )
                low_ref[pl.ds(8, 1), lanes] = low_ref[pl.ds(8, 1), lanes] + (even + odd)
                top_ref[pl.ds(8, 1), lanes] = top_ref[pl.ds(8, 1), lanes] + (even - odd)
        if start + BLOCK == HALF:
            low_ref[pl.ds(8 + HALF, 1), :] = top_ref[pl.ds(7 + HALF, 1), :]
            top_ref[pl.ds(8 + HALF, 1), :] = low_ref[pl.ds(7 + HALF, 1), :]
        ready = start + BLOCK if start + BLOCK == HALF else start + BLOCK - 8
        while done < ready:
            size = min(LANES, ready - done)
            values(done, size)
            done += size
    above = []
    for b in range(HALF // LANES):
        turned = res_ref[pl.ds(LANES * b, LANES), :].T
        peer, at = divmod(LANES * b, out_ref.shape[-1])
        out_ref[peer, :, pl.ds(at, LANES)] = turned[: SLOT * modes]
        above.append(turned[SLOT * modes :])
    high, low = halves_of(jnp.concatenate(above, axis=0))
    above = product(high, flip_ref[...]) + product(low, flip_ref[...])
    for b in range(HALF // LANES):
        peer, at = divmod(NY - LANES * (b + 1), out_ref.shape[-1])
        out_ref[peer, :, pl.ds(at, LANES)] = above[SLOT * modes * b : SLOT * modes * (b + 1)]
    for d, out in enumerate(outs):
        out[...] = out_ref[me_ref[0] ^ d]


def criterion(me, field, high, low, numbers, places, peers):
    modes = field.shape[1] * len(places) // NY
    width = LANES * modes
    fast, slow = pl.BlockSpec(memory_space=pltpu.VMEM), pl.BlockSpec(memory_space=pltpu.HBM)
    call = pl.pallas_call(
        lambda *refs: criterion_kernel(places, peers, *refs),
        in_specs=[pl.BlockSpec(memory_space=pltpu.SMEM), fast, slow, slow, fast, fast, fast, fast],
        out_specs=[fast] * peers,
        out_shape=[jax.ShapeDtypeStruct((SLOT * modes, NY // peers), jnp.float32)] * peers,
        scratch_shapes=[pltpu.VMEM(high.shape, jnp.bfloat16)] * 2
        + [pltpu.VMEM((2, HALF, width), jnp.bfloat16)] * 2
        + [pltpu.VMEM((HALF + 16, width), jnp.float32)] * 2
        + [pltpu.VMEM((HALF, 2 * width), jnp.bfloat16)] * 2
        + [pltpu.VMEM((HALF, LANES), jnp.float32), pltpu.VMEM((peers, SLOT * modes, NY // peers), jnp.float32)]
        + [pltpu.SemaphoreType.DMA((HALF // BLOCK, 2))],
        compiler_params=pltpu.CompilerParams(vmem_limit_bytes=LIMIT),
        name="criterion",
    )
    high, low = (pltpu.with_memory_space_constraint(x, pltpu.HBM) for x in (high, low))
    return call(me[None], field.reshape(NY * modes, LANES), high, low, *numbers)


def local(velocity, vorticity):
    walls = lax.axis_size("gy")
    places = routes()
    columns = NZ // (len(places) * walls)
    sent = pack(velocity, vorticity, places)
    field = lax.all_to_all(sent, ROUTE, split_axis=0, concat_axis=0, tiled=True)
    high, low = tables()
    start = lax.axis_index(SPANS) * columns
    own = (jnp.arange(LANES, dtype=jnp.int32) - start) % LANES
    numbers = factors(own, lax.axis_index("gy") * (NZ // walls) + start)
    me = lax.axis_index("gy")
    parts = criterion(me, field, high, low, numbers, places, walls)
    parts = [parts[0]] + [
        lax.ppermute(parts[d], "gy", [(i, i ^ d) for i in range(walls)]) for d in range(1, walls)
    ]
    blocks = jnp.stack([lax.select_n(me, *(parts[q ^ d] for d in range(walls))) for q in range(walls)])
    blocks = blocks.reshape(walls, KX, SLOT, NY // walls)[:, :, :columns]
    return jnp.moveaxis(blocks, 1, 0)


def solution(mesh):
    fine = Mesh(mesh.devices.reshape(*SIZES.values(), -1), (*SIZES, "gy"))
    placed = P(None, None, SPANS, "gy")
    return jax.shard_map(
        local, mesh=fine, in_specs=(placed, placed), out_specs=placed, check_vma=False
    )
```

```python
import math

import jax
import jax.numpy as jnp
from jax import lax
from jax.experimental import pallas as pl
from jax.experimental.pallas import tpu as pltpu
from jax.sharding import Mesh
from jax.sharding import PartitionSpec as P

NY = 1536
NZ = 7680
KX = 2
HALF = NY // 2
SLOT = 32
LANES = 128
BLOCKS = (256, 512)
LIMIT = 24 * 1024 * 1024
SPANS = ("x", "y", "half", "core")
ROUTE = ("half", "y", "x", "core")
SIZES = {"x": 4, "y": 4, "half": 2, "core": 2}


def routes():
    places = []
    for a in range(math.prod(SIZES.values())):
        rest, at = a, {}
        for name in reversed(SPANS):
            rest, at[name] = divmod(rest, SIZES[name])
        place = 0
        for name in ROUTE:
            place = place * SIZES[name] + at[name]
        places.append(place)
    return places


def spanwise(index):
    signed = jnp.where(index < NZ // 2, index, index - NZ)
    return signed.astype(jnp.float32) * (2.0 / NZ)


def pack_kernel(places, cols, v_hbm, o_hbm, out_hbm, v_buf, o_buf, out_ref, sems):
    _, modes, rows, span = v_buf.shape
    chunks = span // LANES
    copies = []
    for t in range(rows // 8):
        at = pl.ds(8 * t, 8)
        pair = [
            pltpu.make_async_copy(src.at[:, :, at, :], dst.at[:, :, at, :], sems.at[t, f])
            for f, (src, dst) in enumerate(((v_hbm, v_buf), (o_hbm, o_buf)))
        ]
        for copy in pair:
            copy.start()
        copies.append(pair)
    lane = lax.broadcasted_iota(jnp.int32, (8, LANES), 1)
    leaving = []
    for t in range(rows // 8):
        at = pl.ds(8 * t, 8)
        for copy in copies[t]:
            copy.wait()
        turned = {}

        def tile(m, g, k):
            if (m, g, k) not in turned:
                ref = (v_buf, o_buf)[g // 2]
                value = ref[g % 2, m, at, pl.ds(LANES * (k % chunks), LANES)]
                turned[m, g, k] = pltpu.roll(value, SLOT * g, 1) if g else value
            return turned[m, g, k]

        for a, place in enumerate(places):
            k, off = divmod(cols * a, LANES)
            own = (lane - off) & (LANES - 1)
            for m in range(modes):
                merged = [tile(m, 0, k + s) for s in range(2 if off + cols > LANES else 1)]
                for g in range(1, 4):
                    merged = [jnp.where(own >= SLOT * g, tile(m, g, k + s), v) for s, v in enumerate(merged)]
                value = merged[0]
                if len(merged) > 1:
                    value = jnp.where((own & (SLOT - 1)) < LANES - off, value, merged[1])
                out_ref[place, pl.ds(8 * t * modes + m, 8, stride=modes), :] = value
        done = pl.ds(8 * t * modes, 8 * modes)
        leaving.append(pltpu.make_async_copy(out_ref.at[:, done, :], out_hbm.at[:, done, :], sems.at[t, 2]))
        leaving[-1].start()
    for copy in leaving:
        copy.wait()


def pack(velocity, vorticity, places):
    _, modes, rows, span = velocity.shape
    peers = len(places)
    return pl.pallas_call(
        lambda *refs: pack_kernel(places, span // peers, *refs),
        in_specs=[pl.BlockSpec(memory_space=pltpu.HBM)] * 2,
        out_specs=pl.BlockSpec(memory_space=pltpu.HBM),
        out_shape=jax.ShapeDtypeStruct((peers, rows * modes, LANES), jnp.float32),
        scratch_shapes=[pltpu.VMEM(velocity.shape, jnp.float32)] * 2
        + [pltpu.VMEM((peers, rows * modes, LANES), jnp.float32), pltpu.SemaphoreType.DMA((rows // 8, 3))],
        compiler_params=pltpu.CompilerParams(vmem_limit_bytes=LIMIT),
        name="pack",
    )(*(pltpu.with_memory_space_constraint(x, pltpu.HBM) for x in (velocity, vorticity)))


def table_kernel(base_ref, hi_ref, lo_ref):
    rows = 32

    def block(i, carry):
        at = pl.ds(pl.multiple_of(i * rows, rows), rows)
        for parity in range(2):
            c, s, turn_c, turn_s = (base_ref[parity, k, at, :] for k in range(4))
            for q in range(HALF // LANES):
                lanes = pl.ds(LANES * q, LANES)
                hi_ref[parity, at, lanes], lo_ref[parity, at, lanes] = halves_of(c)
                c, s = c * turn_c - s * turn_s, s * turn_c + c * turn_s
        return carry

    lax.fori_loop(0, HALF // rows, block, 0)


def tables():
    point = jnp.arange(HALF, dtype=jnp.int32)[:, None]
    first = 2 * jnp.arange(LANES, dtype=jnp.int32)[None, :]
    turn = jnp.full((1, LANES), 2 * LANES, jnp.int32)

    def angle(degree):
        return (degree * (2 * point + 1) % (4 * NY)).astype(jnp.float32) * (math.pi / (2 * NY))

    degrees = jnp.stack([angle(first), angle(first + 1)])
    turns = jnp.broadcast_to(angle(turn), degrees.shape)
    base = jnp.stack([jnp.cos(degrees), jnp.sin(degrees), jnp.cos(turns), jnp.sin(turns)], axis=1)
    return pl.pallas_call(
        table_kernel,
        out_shape=[jax.ShapeDtypeStruct((2, HALF, HALF), jnp.bfloat16)] * 2,
        compiler_params=pltpu.CompilerParams(vmem_limit_bytes=LIMIT),
        name="tables",
    )(base)


def factors(own, first):
    normal = own < 2 * SLOT
    wave_z = spanwise(first + own % SLOT)
    wave_x = (jnp.arange(KX, dtype=jnp.int32) + 1).astype(jnp.float32) / KX
    wave = wave_x[:, None] * wave_x[:, None] + wave_z[None, :] * wave_z[None, :]
    degree = jnp.arange(NY, dtype=jnp.int32).reshape(HALF, 2).T.astype(jnp.float32)
    scaled = degree * (math.pi / NY)
    stretch = (scaled * jnp.sin(scaled))[:, :, None]
    edge = (-0.5 * scaled * jnp.sin(0.5 * scaled))[:, :, None]
    by_degree = jnp.where(normal, jnp.stack([stretch, edge]), 0.0)
    shift = jnp.where(normal, wave, 1.0)
    size = jnp.where(normal, 0.5 * lax.rsqrt(wave), 0.5)
    slope = jnp.where(normal, 0.0, 0.25 / wave)
    rows = jnp.broadcast_to(jnp.stack([shift * size, size, slope], axis=1)[:, :, None, :], (KX, 3, 8, LANES))
    lane = jnp.arange(LANES, dtype=jnp.int32)
    part = jnp.arange(2 * KX, dtype=jnp.int32)
    pick = (own[None, :, None] % SLOT == lane % SLOT) & (lane // SLOT == part[:, None, None])
    pick = pick.reshape(2 * KX * LANES, LANES)
    flip = lane[:, None] + lane[None, :] == LANES - 1
    return by_degree, rows, pick.astype(jnp.bfloat16), flip.astype(jnp.bfloat16)


def halves_of(value):
    high = value.astype(jnp.bfloat16)
    return high, (value - high.astype(jnp.float32)).astype(jnp.bfloat16)


def product(a, b):
    return jnp.dot(a, b, preferred_element_type=jnp.float32)


def criterion_kernel(
    places, peers, me_ref, x_ref, hi_hbm, lo_hbm, degree_ref, rows_ref, pick_ref, flip_ref, *refs
):
    outs, (hi_ref, lo_ref, xh_ref, xl_ref, low_ref, top_ref, vh_ref, vl_ref, res_ref, out_ref, sems) = (
        refs[:peers],
        refs[peers:],
    )
    copies = [
        [
            pltpu.make_async_copy(src.at[:, at, :], dst.at[:, at, :], sems.at[b, k])
            for k, (src, dst) in enumerate(((hi_hbm, hi_ref), (lo_hbm, lo_ref)))
        ]
        for b, at in enumerate(pl.ds(sum(BLOCKS[:b]), size) for b, size in enumerate(BLOCKS))
    ]
    for copy in sum(copies, []):
        copy.start()
    modes = x_ref.shape[0] // NY
    pair = 2 * NY // len(places)
    half = pair // 2
    totals = [jnp.zeros((half, LANES), jnp.float32) for _ in range(2 * modes)]
    for parity in range(2):
        for m in range(modes):
            lanes = pl.ds(LANES * m, LANES)
            shift, size = rows_ref[m, 0, :1], rows_ref[m, 1, :1]
            for row in range(0, HALF, half):
                at = pl.ds(row, half)
                first = places[2 * row // half] * half * modes + parity * modes + m
                x = x_ref[pl.ds(first, half, stride=2 * modes), :]
                totals[parity * modes + m] = totals[parity * modes + m] + x * degree_ref[1, parity, at, :]
                high, low = halves_of(x * (shift + size * degree_ref[0, parity, at, :]))
                xh_ref[parity, at, lanes] = high
                xl_ref[parity, at, lanes] = low
    outside = jnp.zeros((8, LANES * modes), jnp.float32)
    low_ref[pl.ds(0, 8), :] = outside
    top_ref[pl.ds(0, 8), :] = outside

    def values(start, size):
        at = pl.ds(start, size)
        for part in range(2 * modes):
            ref, m = (low_ref, top_ref)[part // modes], part % modes
            lanes = pl.ds(LANES * m, LANES)
            here = ref[pl.ds(8 + start, size), lanes]
            slope = ref[pl.ds(9 + start, size), lanes] - ref[pl.ds(7 + start, size), lanes]
            high, low = halves_of(here * here + slope * slope * rows_ref[m, 2, :1])
            vh_ref[at, pl.ds(LANES * part, LANES)] = high
            vl_ref[at, pl.ds(LANES * part, LANES)] = low
        res_ref[at, :] = product(vh_ref[at, :], pick_ref[...]) + product(vl_ref[at, :], pick_ref[...])

    done = 0
    for block, rows in enumerate(BLOCKS):
        start = sum(BLOCKS[:block])
        at = pl.ds(start, rows)
        for copy in copies[block]:
            copy.wait()
        halves = []
        for parity in range(2):
            xh = xh_ref[parity]
            halves.append(
                product(hi_ref[parity, at, :], xh) + product(hi_ref[parity, at, :], xl_ref[parity]) + product(lo_ref[parity, at, :], xh)
            )
        low_ref[pl.ds(8 + start, rows), :] = halves[0] + halves[1]
        top_ref[pl.ds(8 + start, rows), :] = halves[0] - halves[1]
        if start == 0:
            for m in range(modes):
                lanes = pl.ds(LANES * m, LANES)
                even, odd = (
                    rows_ref[m, 1, :1] * jnp.sum(totals[parity * modes + m], axis=0, keepdims=True) for parity in range(2)
                )
                low_ref[pl.ds(8, 1), lanes] = low_ref[pl.ds(8, 1), lanes] + (even + odd)
                top_ref[pl.ds(8, 1), lanes] = top_ref[pl.ds(8, 1), lanes] + (even - odd)
        if start + rows == HALF:
            low_ref[pl.ds(8 + HALF, 1), :] = top_ref[pl.ds(7 + HALF, 1), :]
            top_ref[pl.ds(8 + HALF, 1), :] = low_ref[pl.ds(7 + HALF, 1), :]
        ready = start + rows - (8 if start + rows < HALF else 0)
        while done < ready:
            size = min(LANES, ready - done)
            values(done, size)
            done += size
    above = []
    for b in range(HALF // LANES):
        turned = res_ref[pl.ds(LANES * b, LANES), :].T
        peer, at = divmod(LANES * b, out_ref.shape[-1])
        out_ref[peer, :, pl.ds(at, LANES)] = turned[: SLOT * modes]
        above.append(turned[SLOT * modes :])
    high, low = halves_of(jnp.concatenate(above, axis=0))
    above = product(high, flip_ref[...]) + product(low, flip_ref[...])
    for b in range(HALF // LANES):
        peer, at = divmod(NY - LANES * (b + 1), out_ref.shape[-1])
        out_ref[peer, :, pl.ds(at, LANES)] = above[SLOT * modes * b : SLOT * modes * (b + 1)]
    for d, out in enumerate(outs):
        out[...] = out_ref[me_ref[0] ^ d]


def criterion(me, field, high, low, numbers, places, peers):
    modes = field.shape[1] * len(places) // NY
    width = LANES * modes
    fast, slow = pl.BlockSpec(memory_space=pltpu.VMEM), pl.BlockSpec(memory_space=pltpu.HBM)
    call = pl.pallas_call(
        lambda *refs: criterion_kernel(places, peers, *refs),
        in_specs=[pl.BlockSpec(memory_space=pltpu.SMEM), fast, slow, slow, fast, fast, fast, fast],
        out_specs=[fast] * peers,
        out_shape=[pltpu.VMEM((SLOT * modes, NY // peers), jnp.float32)] * peers,
        scratch_shapes=[pltpu.VMEM(high.shape, jnp.bfloat16)] * 2
        + [pltpu.VMEM((2, HALF, width), jnp.bfloat16)] * 2
        + [pltpu.VMEM((HALF + 16, width), jnp.float32)] * 2
        + [pltpu.VMEM((HALF, 2 * width), jnp.bfloat16)] * 2
        + [pltpu.VMEM((HALF, LANES), jnp.float32), pltpu.VMEM((peers, SLOT * modes, NY // peers), jnp.float32)]
        + [pltpu.SemaphoreType.DMA((len(BLOCKS), 2))],
        compiler_params=pltpu.CompilerParams(vmem_limit_bytes=LIMIT),
        name="criterion",
    )
    high, low = (pltpu.with_memory_space_constraint(x, pltpu.HBM) for x in (high, low))
    return call(me[None], field.reshape(NY * modes, LANES), high, low, *numbers)


def assemble_kernel(me_ref, *refs):
    parts, out_ref = refs[:-1], refs[-1]
    modes, columns, senders, _ = out_ref.shape
    for d, part in enumerate(parts):
        for q in range(senders):

            @pl.when((me_ref[0] ^ d) == q)
            def _():
                for m in range(modes):
                    out_ref[m, :, q, :] = part[pl.ds(SLOT * m, columns), :]


def assemble(me, parts, columns):
    modes = parts[0].shape[0] // SLOT
    fast = pl.BlockSpec(memory_space=pltpu.VMEM)
    return pl.pallas_call(
        assemble_kernel,
        in_specs=[pl.BlockSpec(memory_space=pltpu.SMEM)] + [fast] * len(parts),
        out_shape=jax.ShapeDtypeStruct((modes, columns, len(parts), parts[0].shape[1]), jnp.float32),
        compiler_params=pltpu.CompilerParams(vmem_limit_bytes=LIMIT),
        name="assemble",
    )(me[None], *parts)


def local(velocity, vorticity):
    walls = lax.axis_size("gy")
    places = routes()
    columns = NZ // (len(places) * walls)
    sent = pack(velocity, vorticity, places)
    field = lax.all_to_all(sent, ROUTE, split_axis=0, concat_axis=0, tiled=True)
    high, low = tables()
    start = lax.axis_index(SPANS) * columns
    own = (jnp.arange(LANES, dtype=jnp.int32) - start) % LANES
    numbers = factors(own, lax.axis_index("gy") * (NZ // walls) + start)
    me = lax.axis_index("gy")
    parts = criterion(me, field, high, low, numbers, places, walls)
    parts = [parts[0]] + [
        lax.ppermute(parts[d], "gy", [(i, i ^ d) for i in range(walls)]) for d in range(1, walls)
    ]
    return jnp.moveaxis(assemble(me, parts, columns), 2, 1)


def solution(mesh):
    fine = Mesh(mesh.devices.reshape(*SIZES.values(), -1), (*SIZES, "gy"))
    placed = P(None, None, SPANS, "gy")
    return jax.shard_map(
        local, mesh=fine, in_specs=(placed, placed), out_specs=placed, check_vma=False
    )
```

```python
import math

import jax
import jax.numpy as jnp
from jax import lax
from jax.experimental import pallas as pl
from jax.experimental.pallas import tpu as pltpu
from jax.sharding import Mesh
from jax.sharding import PartitionSpec as P


NY = 1536
NZ = 7680
KX = 2
HALF = NY // 2
SLOT = 32
LANES = 128
BLOCKS = (256, 512)
LIMIT = 24 * 1024 * 1024
SPANS = ("x", "y", "half", "core")
ROUTE = ("half", "y", "x", "core")
SIZES = {"x": 4, "y": 4, "half": 2, "core": 2}


def routes():
    places = []
    for a in range(math.prod(SIZES.values())):
        rest, at = a, {}
        for name in reversed(SPANS):
            rest, at[name] = divmod(rest, SIZES[name])
        place = 0
        for name in ROUTE:
            place = place * SIZES[name] + at[name]
        places.append(place)
    return places


def spanwise(index):
    signed = jnp.where(index < NZ // 2, index, index - NZ)
    return signed.astype(jnp.float32) * (2.0 / NZ)


def pack_kernel(places, cols, v_hbm, o_hbm, out_hbm, v_buf, o_buf, out_ref, sems):
    _, modes, rows, span = v_buf.shape
    chunks = span // LANES
    copies = []
    for t in range(rows // 8):
        at = pl.ds(8 * t, 8)
        pair = [
            pltpu.make_async_copy(src.at[:, :, at, :], dst.at[:, :, at, :], sems.at[t, f])
            for f, (src, dst) in enumerate(((v_hbm, v_buf), (o_hbm, o_buf)))
        ]
        for copy in pair:
            copy.start()
        copies.append(pair)
    lane = lax.broadcasted_iota(jnp.int32, (8, LANES), 1)
    leaving = []
    for t in range(rows // 8):
        at = pl.ds(8 * t, 8)
        for copy in copies[t]:
            copy.wait()
        turned = {}

        def tile(m, g, k):
            if (m, g, k) not in turned:
                ref = (v_buf, o_buf)[g // 2]
                value = ref[g % 2, m, at, pl.ds(LANES * (k % chunks), LANES)]
                turned[m, g, k] = pltpu.roll(value, SLOT * g, 1) if g else value
            return turned[m, g, k]

        for a, place in enumerate(places):
            k, off = divmod(cols * a, LANES)
            own = (lane - off) & (LANES - 1)
            for m in range(modes):
                merged = [tile(m, 0, k + s) for s in range(2 if off + cols > LANES else 1)]
                for g in range(1, 4):
                    merged = [jnp.where(own >= SLOT * g, tile(m, g, k + s), v) for s, v in enumerate(merged)]
                value = merged[0]
                if len(merged) > 1:
                    value = jnp.where((own & (SLOT - 1)) < LANES - off, value, merged[1])
                out_ref[place, pl.ds(8 * t * modes + m, 8, stride=modes), :] = value
        done = pl.ds(8 * t * modes, 8 * modes)
        leaving.append(pltpu.make_async_copy(out_ref.at[:, done, :], out_hbm.at[:, done, :], sems.at[t, 2]))
        leaving[-1].start()
    for copy in leaving:
        copy.wait()


def pack(velocity, vorticity, places):
    _, modes, rows, span = velocity.shape
    peers = len(places)
    return pl.pallas_call(
        lambda *refs: pack_kernel(places, span // peers, *refs),
        in_specs=[pl.BlockSpec(memory_space=pltpu.HBM)] * 2,
        out_specs=pl.BlockSpec(memory_space=pltpu.HBM),
        out_shape=jax.ShapeDtypeStruct((peers, rows * modes, LANES), jnp.float32),
        scratch_shapes=[pltpu.VMEM(velocity.shape, jnp.float32)] * 2
        + [pltpu.VMEM((peers, rows * modes, LANES), jnp.float32), pltpu.SemaphoreType.DMA((rows // 8, 3))],
        compiler_params=pltpu.CompilerParams(vmem_limit_bytes=LIMIT),
        name="pack",
    )(*(pltpu.with_memory_space_constraint(x, pltpu.HBM) for x in (velocity, vorticity)))


def table_kernel(base_ref, hi_ref, lo_ref):
    rows = 32

    def block(i, carry):
        at = pl.ds(pl.multiple_of(i * rows, rows), rows)
        for parity in range(2):
            c, s, turn_c, turn_s = (base_ref[parity, k, at, :] for k in range(4))
            for q in range(HALF // LANES):
                lanes = pl.ds(LANES * q, LANES)
                hi_ref[parity, at, lanes], lo_ref[parity, at, lanes] = halves_of(c)
                c, s = c * turn_c - s * turn_s, s * turn_c + c * turn_s
        return carry

    lax.fori_loop(0, HALF // rows, block, 0)


def tables():
    point = jnp.arange(HALF, dtype=jnp.int32)[:, None]
    first = 2 * jnp.arange(LANES, dtype=jnp.int32)[None, :]
    turn = jnp.full((1, LANES), 2 * LANES, jnp.int32)

    def angle(degree):
        return (degree * (2 * point + 1) % (4 * NY)).astype(jnp.float32) * (math.pi / (2 * NY))

    degrees = jnp.stack([angle(first), angle(first + 1)])
    turns = jnp.broadcast_to(angle(turn), degrees.shape)
    base = jnp.stack([jnp.cos(degrees), jnp.sin(degrees), jnp.cos(turns), jnp.sin(turns)], axis=1)
    return pl.pallas_call(
        table_kernel,
        out_shape=[jax.ShapeDtypeStruct((2, HALF, HALF), jnp.bfloat16)] * 2,
        compiler_params=pltpu.CompilerParams(vmem_limit_bytes=LIMIT),
        name="tables",
    )(base)


def factors(own, first):
    normal = own < 2 * SLOT
    wave_z = spanwise(first + own % SLOT)
    wave_x = (jnp.arange(KX, dtype=jnp.int32) + 1).astype(jnp.float32) / KX
    wave = wave_x[:, None] * wave_x[:, None] + wave_z[None, :] * wave_z[None, :]
    degree = jnp.arange(NY, dtype=jnp.int32).reshape(HALF, 2).T.astype(jnp.float32)
    scaled = degree * (math.pi / NY)
    stretch = (scaled * jnp.sin(scaled))[:, :, None]
    edge = (-0.5 * scaled * jnp.sin(0.5 * scaled))[:, :, None]
    by_degree = jnp.where(normal, jnp.stack([stretch, edge]), 0.0)
    shift = jnp.where(normal, wave, 1.0)
    size = jnp.where(normal, 0.5 * lax.rsqrt(wave), 0.5)
    slope = jnp.where(normal, 0.0, 0.25 / wave)
    rows = jnp.broadcast_to(jnp.stack([shift * size, size, slope], axis=1)[:, :, None, :], (KX, 3, 8, LANES))
    lane = jnp.arange(LANES, dtype=jnp.int32)
    part = jnp.arange(2 * KX, dtype=jnp.int32)
    pick = (own[None, :, None] % SLOT == lane % SLOT) & (lane // SLOT == part[:, None, None])
    pick = pick.reshape(2 * KX * LANES, LANES)
    flip = lane[:, None] + lane[None, :] == LANES - 1
    return by_degree, rows, pick.astype(jnp.bfloat16), flip.astype(jnp.bfloat16)


def halves_of(value):
    high = value.astype(jnp.bfloat16)
    return high, (value - high.astype(jnp.float32)).astype(jnp.bfloat16)


def product(a, b):
    return jnp.dot(a, b, preferred_element_type=jnp.float32)


def criterion_kernel(
    places, peers, me_ref, x_ref, hi_hbm, lo_hbm, degree_ref, rows_ref, pick_ref, flip_ref, *refs
):
    outs, (hi_ref, lo_ref, xh_ref, xl_ref, low_ref, top_ref, vh_ref, vl_ref, res_ref, out_ref, sems) = (
        refs[:peers],
        refs[peers:],
    )
    copies = [
        [
            pltpu.make_async_copy(src.at[:, at, :], dst.at[:, at, :], sems.at[b, k])
            for k, (src, dst) in enumerate(((hi_hbm, hi_ref), (lo_hbm, lo_ref)))
        ]
        for b, at in enumerate(pl.ds(sum(BLOCKS[:b]), size) for b, size in enumerate(BLOCKS))
    ]
    for copy in sum(copies, []):
        copy.start()
    modes = x_ref.shape[0] // NY
    pair = 2 * NY // len(places)
    half = pair // 2
    totals = [jnp.zeros((half, LANES), jnp.float32) for _ in range(2 * modes)]
    for parity in range(2):
        for m in range(modes):
            lanes = pl.ds(LANES * m, LANES)
            shift, size = rows_ref[m, 0, :1], rows_ref[m, 1, :1]
            for row in range(0, HALF, half):
                at = pl.ds(row, half)
                first = places[2 * row // half] * half * modes + parity * modes + m
                x = x_ref[pl.ds(first, half, stride=2 * modes), :]
                totals[parity * modes + m] = totals[parity * modes + m] + x * degree_ref[1, parity, at, :]
                high, low = halves_of(x * (shift + size * degree_ref[0, parity, at, :]))
                xh_ref[parity, at, lanes] = high
                xl_ref[parity, at, lanes] = low
    outside = jnp.zeros((8, LANES * modes), jnp.float32)
    low_ref[pl.ds(0, 8), :] = outside
    top_ref[pl.ds(0, 8), :] = outside

    def values(start, size):
        at = pl.ds(start, size)
        for part in range(2 * modes):
            ref, m = (low_ref, top_ref)[part // modes], part % modes
            lanes = pl.ds(LANES * m, LANES)
            here = ref[pl.ds(8 + start, size), lanes]
            slope = ref[pl.ds(9 + start, size), lanes] - ref[pl.ds(7 + start, size), lanes]
            high, low = halves_of(here * here + slope * slope * rows_ref[m, 2, :1])
            vh_ref[at, pl.ds(LANES * part, LANES)] = high
            vl_ref[at, pl.ds(LANES * part, LANES)] = low
        res_ref[at, :] = product(vh_ref[at, :], pick_ref[...]) + product(vl_ref[at, :], pick_ref[...])

    done = 0
    for block, rows in enumerate(BLOCKS):
        start = sum(BLOCKS[:block])
        at = pl.ds(start, rows)
        for copy in copies[block]:
            copy.wait()
        halves = []
        for parity in range(2):
            xh = xh_ref[parity]
            halves.append(
                product(hi_ref[parity, at, :], xh) + product(hi_ref[parity, at, :], xl_ref[parity]) + product(lo_ref[parity, at, :], xh)
            )
        low_ref[pl.ds(8 + start, rows), :] = halves[0] + halves[1]
        top_ref[pl.ds(8 + start, rows), :] = halves[0] - halves[1]
        if start == 0:
            for m in range(modes):
                lanes = pl.ds(LANES * m, LANES)
                even, odd = (
                    rows_ref[m, 1, :1] * jnp.sum(totals[parity * modes + m], axis=0, keepdims=True) for parity in range(2)
                )
                low_ref[pl.ds(8, 1), lanes] = low_ref[pl.ds(8, 1), lanes] + (even + odd)
                top_ref[pl.ds(8, 1), lanes] = top_ref[pl.ds(8, 1), lanes] + (even - odd)
        if start + rows == HALF:
            low_ref[pl.ds(8 + HALF, 1), :] = top_ref[pl.ds(7 + HALF, 1), :]
            top_ref[pl.ds(8 + HALF, 1), :] = low_ref[pl.ds(7 + HALF, 1), :]
        ready = start + rows - (8 if start + rows < HALF else 0)
        while done < ready:
            size = min(LANES, ready - done)
            values(done, size)
            done += size
    above = []
    for b in range(HALF // LANES):
        turned = res_ref[pl.ds(LANES * b, LANES), :].T
        peer, at = divmod(LANES * b, out_ref.shape[-1])
        out_ref[peer, :, pl.ds(at, LANES)] = turned[: SLOT * modes]
        above.append(turned[SLOT * modes :])
    high, low = halves_of(jnp.concatenate(above, axis=0))
    above = product(high, flip_ref[...]) + product(low, flip_ref[...])
    for b in range(HALF // LANES):
        peer, at = divmod(NY - LANES * (b + 1), out_ref.shape[-1])
        out_ref[peer, :, pl.ds(at, LANES)] = above[SLOT * modes * b : SLOT * modes * (b + 1)]
    for d, out in enumerate(outs):
        out[...] = out_ref[me_ref[0] ^ d]


def criterion(me, field, high, low, numbers, places, peers):
    modes = field.shape[1] * len(places) // NY
    width = LANES * modes
    fast, slow = pl.BlockSpec(memory_space=pltpu.VMEM), pl.BlockSpec(memory_space=pltpu.HBM)
    call = pl.pallas_call(
        lambda *refs: criterion_kernel(places, peers, *refs),
        in_specs=[pl.BlockSpec(memory_space=pltpu.SMEM), fast, slow, slow, fast, fast, fast, fast],
        out_specs=[fast] * peers,
        out_shape=[pltpu.VMEM((SLOT * modes, NY // peers), jnp.float32)] * peers,
        scratch_shapes=[pltpu.VMEM(high.shape, jnp.bfloat16)] * 2
        + [pltpu.VMEM((2, HALF, width), jnp.bfloat16)] * 2
        + [pltpu.VMEM((HALF + 16, width), jnp.float32)] * 2
        + [pltpu.VMEM((HALF, 2 * width), jnp.bfloat16)] * 2
        + [pltpu.VMEM((HALF, LANES), jnp.float32), pltpu.VMEM((peers, SLOT * modes, NY // peers), jnp.float32)]
        + [pltpu.SemaphoreType.DMA((len(BLOCKS), 2))],
        compiler_params=pltpu.CompilerParams(vmem_limit_bytes=LIMIT),
        name="criterion",
    )
    high, low = (pltpu.with_memory_space_constraint(x, pltpu.HBM) for x in (high, low))
    return call(me[None], field.reshape(NY * modes, LANES), high, low, *numbers)


def assemble_kernel(me_ref, *refs):
    parts, out_ref = refs[:-1], refs[-1]
    modes, columns, senders, _ = out_ref.shape
    for d, part in enumerate(parts):
        for q in range(senders):

            @pl.when((me_ref[0] ^ d) == q)
            def _():
                for m in range(modes):
                    out_ref[m, :, q, :] = part[pl.ds(SLOT * m, columns), :]


def assemble(me, parts, columns):
    modes = parts[0].shape[0] // SLOT
    fast = pl.BlockSpec(memory_space=pltpu.VMEM)
    return pl.pallas_call(
        assemble_kernel,
        in_specs=[pl.BlockSpec(memory_space=pltpu.SMEM)] + [fast] * len(parts),
        out_shape=jax.ShapeDtypeStruct((modes, columns, len(parts), parts[0].shape[1]), jnp.float32),
        compiler_params=pltpu.CompilerParams(vmem_limit_bytes=LIMIT),
        name="assemble",
    )(me[None], *parts)


def local(velocity, vorticity):
    walls = lax.axis_size("gy")
    places = routes()
    columns = NZ // (len(places) * walls)
    sent = pack(velocity, vorticity, places)
    field = lax.all_to_all(sent, ROUTE, split_axis=0, concat_axis=0, tiled=True)
    high, low = tables()
    start = lax.axis_index(SPANS) * columns
    own = (jnp.arange(LANES, dtype=jnp.int32) - start) % LANES
    numbers = factors(own, lax.axis_index("gy") * (NZ // walls) + start)
    me = lax.axis_index("gy")
    parts = list(criterion(me, field, high, low, numbers, places, walls))
    for d in range(1, walls):
        parts[d] = lax.ppermute(parts[d], "gy", [(i, i ^ d) for i in range(walls)])
    return jnp.moveaxis(assemble(me, parts, columns), 2, 1)


def solution(mesh):
    fine = Mesh(mesh.devices.reshape(*SIZES.values(), -1), (*SIZES, "gy"))
    placed = P(None, None, SPANS, "gy")
    return jax.shard_map(
        local, mesh=fine, in_specs=(placed, placed), out_specs=placed, check_vma=False
    )
```

```python
import math

import jax
import jax.numpy as jnp
from jax import lax
from jax.experimental import pallas as pl
from jax.experimental.pallas import tpu as pltpu
from jax.sharding import Mesh
from jax.sharding import PartitionSpec as P


NY = 1536
NZ = 7680
KX = 2
HALF = NY // 2
SLOT = 32
LANES = 128
BLOCKS = (256, 512)
LIMIT = 24 * 1024 * 1024
SPANS = ("x", "y", "half", "core")
ROUTE = ("half", "y", "x", "core")
SIZES = {"x": 4, "y": 4, "half": 2, "core": 2}


def routes():
    places = []
    for a in range(math.prod(SIZES.values())):
        rest, at = a, {}
        for name in reversed(SPANS):
            rest, at[name] = divmod(rest, SIZES[name])
        place = 0
        for name in ROUTE:
            place = place * SIZES[name] + at[name]
        places.append(place)
    return places


def spanwise(index):
    signed = jnp.where(index < NZ // 2, index, index - NZ)
    return signed.astype(jnp.float32) * (2.0 / NZ)


def pack_kernel(places, cols, v_hbm, o_hbm, out_hbm, v_buf, o_buf, out_ref, sems):
    _, modes, rows, span = v_buf.shape
    chunks = span // LANES
    copies = []
    for t in range(rows // 8):
        at = pl.ds(8 * t, 8)
        pair = [
            pltpu.make_async_copy(src.at[:, :, at, :], dst.at[:, :, at, :], sems.at[t, f])
            for f, (src, dst) in enumerate(((v_hbm, v_buf), (o_hbm, o_buf)))
        ]
        for copy in pair:
            copy.start()
        copies.append(pair)
    lane = lax.broadcasted_iota(jnp.int32, (8, LANES), 1)
    leaving = []
    for t in range(rows // 8):
        at = pl.ds(8 * t, 8)
        for copy in copies[t]:
            copy.wait()
        turned = {}

        def tile(m, g, k):
            if (m, g, k) not in turned:
                ref = (v_buf, o_buf)[g // 2]
                value = ref[g % 2, m, at, pl.ds(LANES * (k % chunks), LANES)]
                turned[m, g, k] = pltpu.roll(value, SLOT * g, 1) if g else value
            return turned[m, g, k]

        for a, place in enumerate(places):
            k, off = divmod(cols * a, LANES)
            own = (lane - off) & (LANES - 1)
            for m in range(modes):
                merged = [tile(m, 0, k + s) for s in range(2 if off + cols > LANES else 1)]
                for g in range(1, 4):
                    merged = [jnp.where(own >= SLOT * g, tile(m, g, k + s), v) for s, v in enumerate(merged)]
                value = merged[0]
                if len(merged) > 1:
                    value = jnp.where((own & (SLOT - 1)) < LANES - off, value, merged[1])
                out_ref[place, pl.ds(8 * t * modes + m, 8, stride=modes), :] = value
        done = pl.ds(8 * t * modes, 8 * modes)
        leaving.append(pltpu.make_async_copy(out_ref.at[:, done, :], out_hbm.at[:, done, :], sems.at[t, 2]))
        leaving[-1].start()
    for copy in leaving:
        copy.wait()


def pack(velocity, vorticity, places):
    _, modes, rows, span = velocity.shape
    peers = len(places)
    return pl.pallas_call(
        lambda *refs: pack_kernel(places, span // peers, *refs),
        in_specs=[pl.BlockSpec(memory_space=pltpu.HBM)] * 2,
        out_specs=pl.BlockSpec(memory_space=pltpu.HBM),
        out_shape=jax.ShapeDtypeStruct((peers, rows * modes, LANES), jnp.float32),
        scratch_shapes=[pltpu.VMEM(velocity.shape, jnp.float32)] * 2
        + [pltpu.VMEM((peers, rows * modes, LANES), jnp.float32), pltpu.SemaphoreType.DMA((rows // 8, 3))],
        compiler_params=pltpu.CompilerParams(vmem_limit_bytes=LIMIT),
        name="pack",
    )(*(pltpu.with_memory_space_constraint(x, pltpu.HBM) for x in (velocity, vorticity)))


def table_kernel(base_ref, hi_ref, lo_ref):
    rows = 32

    def block(i, carry):
        at = pl.ds(pl.multiple_of(i * rows, rows), rows)
        for parity in range(2):
            c, s, turn_c, turn_s = (base_ref[parity, k, at, :] for k in range(4))
            for q in range(HALF // LANES):
                lanes = pl.ds(LANES * q, LANES)
                hi_ref[parity, at, lanes], lo_ref[parity, at, lanes] = halves_of(c)
                c, s = c * turn_c - s * turn_s, s * turn_c + c * turn_s
        return carry

    lax.fori_loop(0, HALF // rows, block, 0)


def tables():
    point = jnp.arange(HALF, dtype=jnp.int32)[:, None]
    first = 2 * jnp.arange(LANES, dtype=jnp.int32)[None, :]
    turn = jnp.full((1, LANES), 2 * LANES, jnp.int32)

    def angle(degree):
        return (degree * (2 * point + 1) % (4 * NY)).astype(jnp.float32) * (math.pi / (2 * NY))

    degrees = jnp.stack([angle(first), angle(first + 1)])
    turns = jnp.broadcast_to(angle(turn), degrees.shape)
    base = jnp.stack([jnp.cos(degrees), jnp.sin(degrees), jnp.cos(turns), jnp.sin(turns)], axis=1)
    return pl.pallas_call(
        table_kernel,
        out_shape=[jax.ShapeDtypeStruct((2, HALF, HALF), jnp.bfloat16)] * 2,
        compiler_params=pltpu.CompilerParams(vmem_limit_bytes=LIMIT),
        name="tables",
    )(base)


def factors(own, first, columns):
    normal = own < 2 * SLOT
    wave_z = spanwise(first + own % SLOT)
    wave_x = (jnp.arange(KX, dtype=jnp.int32) + 1).astype(jnp.float32) / KX
    wave = wave_x[:, None] * wave_x[:, None] + wave_z[None, :] * wave_z[None, :]
    degree = jnp.arange(NY, dtype=jnp.int32).reshape(HALF, 2).T.astype(jnp.float32)
    scaled = degree * (math.pi / NY)
    stretch = (scaled * jnp.sin(scaled))[:, :, None]
    edge = (-0.5 * scaled * jnp.sin(0.5 * scaled))[:, :, None]
    by_degree = jnp.where(normal, jnp.stack([stretch, edge]), 0.0)
    shift = jnp.where(normal, wave, 1.0)
    size = jnp.where(normal, 0.5 * lax.rsqrt(wave), 0.5)
    slope = jnp.where(normal, 0.0, 0.25 / wave)
    rows = jnp.broadcast_to(jnp.stack([shift * size, size, slope], axis=1)[:, :, None, :], (KX, 3, 8, LANES))
    lane = jnp.arange(LANES, dtype=jnp.int32)
    part = jnp.arange(2 * KX, dtype=jnp.int32)
    target = part[:, None] // KX * (SLOT * KX) + part[:, None] % KX * columns + own % SLOT
    pick = (target[:, :, None] == lane) & (own % SLOT < columns)[None, :, None]
    pick = pick.reshape(2 * KX * LANES, LANES)
    flip = lane[:, None] + lane[None, :] == LANES - 1
    return by_degree, rows, pick.astype(jnp.bfloat16), flip.astype(jnp.bfloat16)


def halves_of(value):
    high = value.astype(jnp.bfloat16)
    return high, (value - high.astype(jnp.float32)).astype(jnp.bfloat16)


def product(a, b):
    return jnp.dot(a, b, preferred_element_type=jnp.float32)


def criterion_kernel(
    places, peers, me_ref, x_ref, hi_hbm, lo_hbm, degree_ref, rows_ref, pick_ref, flip_ref, *refs
):
    outs, (hi_ref, lo_ref, xh_ref, xl_ref, low_ref, top_ref, vh_ref, vl_ref, res_ref, out_ref, sems) = (
        refs[:peers],
        refs[peers:],
    )
    copies = [
        [
            pltpu.make_async_copy(src.at[:, at, :], dst.at[:, at, :], sems.at[b, k])
            for k, (src, dst) in enumerate(((hi_hbm, hi_ref), (lo_hbm, lo_ref)))
        ]
        for b, at in enumerate(pl.ds(sum(BLOCKS[:b]), size) for b, size in enumerate(BLOCKS))
    ]
    for copy in sum(copies, []):
        copy.start()
    modes = x_ref.shape[0] // NY
    pair = 2 * NY // len(places)
    half = pair // 2
    totals = [jnp.zeros((half, LANES), jnp.float32) for _ in range(2 * modes)]
    for parity in range(2):
        for m in range(modes):
            lanes = pl.ds(LANES * m, LANES)
            shift, size = rows_ref[m, 0, :1], rows_ref[m, 1, :1]
            for row in range(0, HALF, half):
                at = pl.ds(row, half)
                first = places[2 * row // half] * half * modes + parity * modes + m
                x = x_ref[pl.ds(first, half, stride=2 * modes), :]
                totals[parity * modes + m] = totals[parity * modes + m] + x * degree_ref[1, parity, at, :]
                high, low = halves_of(x * (shift + size * degree_ref[0, parity, at, :]))
                xh_ref[parity, at, lanes] = high
                xl_ref[parity, at, lanes] = low
    outside = jnp.zeros((8, LANES * modes), jnp.float32)
    low_ref[pl.ds(0, 8), :] = outside
    top_ref[pl.ds(0, 8), :] = outside

    def values(start, size):
        at = pl.ds(start, size)
        for part in range(2 * modes):
            ref, m = (low_ref, top_ref)[part // modes], part % modes
            lanes = pl.ds(LANES * m, LANES)
            here = ref[pl.ds(8 + start, size), lanes]
            slope = ref[pl.ds(9 + start, size), lanes] - ref[pl.ds(7 + start, size), lanes]
            high, low = halves_of(here * here + slope * slope * rows_ref[m, 2, :1])
            vh_ref[at, pl.ds(LANES * part, LANES)] = high
            vl_ref[at, pl.ds(LANES * part, LANES)] = low
        res_ref[at, :] = product(vh_ref[at, :], pick_ref[...]) + product(vl_ref[at, :], pick_ref[...])

    done = 0
    for block, rows in enumerate(BLOCKS):
        start = sum(BLOCKS[:block])
        at = pl.ds(start, rows)
        for copy in copies[block]:
            copy.wait()
        halves = []
        for parity in range(2):
            xh = xh_ref[parity]
            halves.append(
                product(hi_ref[parity, at, :], xh) + product(hi_ref[parity, at, :], xl_ref[parity]) + product(lo_ref[parity, at, :], xh)
            )
        low_ref[pl.ds(8 + start, rows), :] = halves[0] + halves[1]
        top_ref[pl.ds(8 + start, rows), :] = halves[0] - halves[1]
        if start == 0:
            for m in range(modes):
                lanes = pl.ds(LANES * m, LANES)
                even, odd = (
                    rows_ref[m, 1, :1] * jnp.sum(totals[parity * modes + m], axis=0, keepdims=True) for parity in range(2)
                )
                low_ref[pl.ds(8, 1), lanes] = low_ref[pl.ds(8, 1), lanes] + (even + odd)
                top_ref[pl.ds(8, 1), lanes] = top_ref[pl.ds(8, 1), lanes] + (even - odd)
        if start + rows == HALF:
            low_ref[pl.ds(8 + HALF, 1), :] = top_ref[pl.ds(7 + HALF, 1), :]
            top_ref[pl.ds(8 + HALF, 1), :] = low_ref[pl.ds(7 + HALF, 1), :]
        ready = start + rows - (8 if start + rows < HALF else 0)
        while done < ready:
            size = min(LANES, ready - done)
            values(done, size)
            done += size
    sent = modes * (NZ // (len(places) * peers))
    above = []
    for b in range(HALF // LANES):
        turned = res_ref[pl.ds(LANES * b, LANES), :].T
        peer, at = divmod(LANES * b, NY // peers)
        out_ref[peer, pl.ds(at // LANES * sent, sent), :] = turned[:sent]
        above.append(turned[SLOT * modes :])
    high, low = halves_of(jnp.concatenate(above, axis=0))
    above = product(high, flip_ref[...]) + product(low, flip_ref[...])
    for b in range(HALF // LANES):
        peer, at = divmod(NY - LANES * (b + 1), NY // peers)
        out_ref[peer, pl.ds(at // LANES * sent, sent), :] = above[SLOT * modes * b : SLOT * modes * b + sent]
    for d, out in enumerate(outs):
        out[...] = out_ref[me_ref[0] ^ d]


def criterion(me, field, high, low, numbers, places, peers):
    points = NY // peers // LANES
    modes = field.shape[1] * len(places) // NY
    width = LANES * modes
    sent = -(-points * modes * (NZ // (len(places) * peers)) // 8) * 8
    fast, slow = pl.BlockSpec(memory_space=pltpu.VMEM), pl.BlockSpec(memory_space=pltpu.HBM)
    call = pl.pallas_call(
        lambda *refs: criterion_kernel(places, peers, *refs),
        in_specs=[pl.BlockSpec(memory_space=pltpu.SMEM), fast, slow, slow, fast, fast, fast, fast],
        out_specs=[fast] * peers,
        out_shape=[pltpu.VMEM((sent, LANES), jnp.float32)] * peers,
        scratch_shapes=[pltpu.VMEM(high.shape, jnp.bfloat16)] * 2
        + [pltpu.VMEM((2, HALF, width), jnp.bfloat16)] * 2
        + [pltpu.VMEM((HALF + 16, width), jnp.float32)] * 2
        + [pltpu.VMEM((HALF, 2 * width), jnp.bfloat16)] * 2
        + [pltpu.VMEM((HALF, LANES), jnp.float32), pltpu.VMEM((peers, sent, LANES), jnp.float32)]
        + [pltpu.SemaphoreType.DMA((len(BLOCKS), 2))],
        compiler_params=pltpu.CompilerParams(vmem_limit_bytes=LIMIT),
        name="criterion",
    )
    high, low = (pltpu.with_memory_space_constraint(x, pltpu.HBM) for x in (high, low))
    return call(me[None], field.reshape(NY * modes, LANES), high, low, *numbers)


def assemble_kernel(me_ref, *refs):
    parts, out_ref = refs[:-1], refs[-1]
    modes, columns, senders, points = out_ref.shape
    for d, part in enumerate(parts):
        for q in range(senders):

            @pl.when((me_ref[0] ^ d) == q)
            def _():
                for m in range(modes):
                    for t in range(points // LANES):
                        out_ref[m, :, q, pl.ds(LANES * t, LANES)] = part[pl.ds((modes * t + m) * columns, columns), :]


def assemble(me, parts, columns):
    points = NY // len(parts)
    fast = pl.BlockSpec(memory_space=pltpu.VMEM)
    return pl.pallas_call(
        assemble_kernel,
        in_specs=[pl.BlockSpec(memory_space=pltpu.SMEM)] + [fast] * len(parts),
        out_shape=jax.ShapeDtypeStruct((KX, columns, len(parts), points), jnp.float32),
        compiler_params=pltpu.CompilerParams(vmem_limit_bytes=LIMIT),
        name="assemble",
    )(me[None], *parts)


def local(velocity, vorticity):
    walls = lax.axis_size("gy")
    places = routes()
    columns = NZ // (len(places) * walls)
    sent = pack(velocity, vorticity, places)
    field = lax.all_to_all(sent, ROUTE, split_axis=0, concat_axis=0, tiled=True)
    high, low = tables()
    start = lax.axis_index(SPANS) * columns
    own = (jnp.arange(LANES, dtype=jnp.int32) - start) % LANES
    numbers = factors(own, lax.axis_index("gy") * (NZ // walls) + start, columns)
    me = lax.axis_index("gy")
    parts = list(criterion(me, field, high, low, numbers, places, walls))
    for d in range(1, walls):
        parts[d] = lax.ppermute(parts[d], "gy", [(i, i ^ d) for i in range(walls)])
    return jnp.moveaxis(assemble(me, parts, columns), 2, 1)


def solution(mesh):
    fine = Mesh(mesh.devices.reshape(*SIZES.values(), -1), (*SIZES, "gy"))
    placed = P(None, None, SPANS, "gy")
    return jax.shard_map(
        local, mesh=fine, in_specs=(placed, placed), out_specs=placed, check_vma=False
    )
```
